512 devices in a mesh: space: 64 (over x, z), knot: 8 (over y, core).
Axes of the slice: x: 4, y: 4, z: 16, core: 2. Of those that a mesh axis runs over, the one named last changes fastest.
Arguments:
- probes: float32 [16, 524288], P(None, ('space', 'knot')), may hold values from -6 to 6
- locations: float32 [2, 524288], P(None, ('space', 'knot')), may hold values from 0 to 6.4, as said below
- knot_locs: float32 [2, 2048], P(None, 'knot'), may hold values from 0 to 6.4, as said below
- knot_precision: float32 [2048, 2048], P('knot'), may hold values from -0.125 to 0.125
- neighbours: int32 [4096, 8], P(('space', 'knot')), may hold values from 0 to 4095, as said below
- counts: int32 [4096], P(('space', 'knot')), may hold values from 1 to 8
Outputs:
- applied: float32 [16, 524288], P(None, ('space', 'knot'))
The draws below stay inside these ranges and needn't reach their ends.
Inputs may be any that keep to these rules, and one draw needn't show every extreme that they name: `locations`: block b lies in one cell of a grid of 64 x 64 cells of side 0.1: its east coordinates in [0.1 (b // 64), 0.1 (b // 64 + 1)], its north ones in [0.1 (b % 64), 0.1 (b % 64 + 1)]. `knot_locs`: knots lie in [0, 0.1 * 64] east and [0, 0.1 * 64] north. neighbours[b, 0] = b; every other entry of row b is the block of one of the eight cells around b's cell, where a step off the grid is turned back in that direction; the steps of a row are distinct.
All inputs are finite; a program needn't handle non-finite values.
Results may differ from the reference program's by a relative error of at most 0.0003.
Values sent between devices are 32-bit elements; how exact they have to be, the bound alone decides.
A program may use at most 64 MiB of HBM per device.

```python
import math
import jax
import jax.numpy as jnp
from jax import lax

NBD = 8
BLOCK = 128
PROBES = 16
KNOTS = 2048
KNB = 8
NCOLS = 64
NROWS = 64
NB = 4096
NOBS = 524288


def draw_locations(key, part):
    split_keys = jax.random.split(jax.random.fold_in(key, 11), 2)
    total = NB * BLOCK
    blocks = jnp.arange(total, dtype=jnp.int32) // BLOCK
    east_cell = (blocks // NROWS).astype(jnp.float32)
    north_cell = (blocks % NROWS).astype(jnp.float32)
    east = (east_cell + jax.random.uniform(split_keys[0], (total,), jnp.float32)) * 0.1
    north = (north_cell + jax.random.uniform(split_keys[1], (total,), jnp.float32)) * 0.1
    return jnp.stack([east, north]).astype(jnp.float32)


def draw_knot_locs(key, part):
    split_keys = jax.random.split(jax.random.fold_in(key, 23), 2)
    east = jax.random.uniform(split_keys[0], (KNOTS,), jnp.float32) * (NCOLS * 0.1)
    north = jax.random.uniform(split_keys[1], (KNOTS,), jnp.float32) * (NROWS * 0.1)
    return jnp.stack([east, north]).astype(jnp.float32)


def draw_neighbours(key, part):
    steps_east = jnp.array([-1, -1, -1, 0, 0, 1, 1, 1], dtype=jnp.int32)
    steps_north = jnp.array([-1, 0, 1, -1, 1, -1, 0, 1], dtype=jnp.int32)
    key_list = jax.random.split(jax.random.fold_in(key, 37), NB)
    shuffled = jax.vmap(lambda single: jax.random.permutation(single, 8))(key_list)
    chosen = shuffled[:, :KNB - 1].astype(jnp.int32)
    blocks = jnp.arange(NB, dtype=jnp.int32)[:, None]
    east_cell = blocks // NROWS
    north_cell = blocks % NROWS
    move_east = steps_east[chosen]
    move_north = steps_north[chosen]
    target_east = east_cell + move_east
    target_east = jnp.where((target_east < 0) | (target_east >= NCOLS), east_cell - move_east, target_east)
    target_north = north_cell + move_north
    target_north = jnp.where((target_north < 0) | (target_north >= NROWS), north_cell - move_north, target_north)
    target = target_east * NROWS + target_north
    return jnp.concatenate([blocks, target], axis=1).astype(jnp.int32)


def draw_counts(key, part):
    values = jax.random.randint(jax.random.fold_in(key, 53), (NB,), 1, KNB + 1, dtype=jnp.int32)
    return values.at[0].set(KNB).at[1].set(1)


def levels(stream_key, shape, cuts, smallest, top_value):
    level, own = 1.0, jax.random.fold_in(stream_key, 6)
    for dim, blocks in cuts:
        heights = jnp.exp(jax.random.uniform(jax.random.fold_in(own, dim), (blocks,), jnp.float32, smallest / len(cuts), top_value / len(cuts)))
        level = level * jnp.repeat(heights, shape[dim] // blocks).reshape([-1 if axis == dim else 1 for axis in range(len(shape))])
    return level


def normal_values(own_key, dims, width, limit, shards=(), kind=jnp.bfloat16):
    values = width * jax.random.normal(own_key, dims, jnp.float32)
    if shards:
        values = values * levels(own_key, dims, shards, -0.22, 0.18)
    return jnp.clip(values, -limit, limit).astype(kind)


def setup_inputs(seed: int = 0) -> dict:
    streams_of = jax.random.split(jax.random.key(seed), 7)
    return {
        "probes": normal_values(streams_of[0], (PROBES, NOBS), 1.0, 6.0, ((1, 512),), jnp.float32),
        "locations": draw_locations(jax.random.fold_in(streams_of[6], 71), 0),
        "knot_locs": draw_knot_locs(jax.random.fold_in(streams_of[6], 71), 0),
        "knot_precision": normal_values(streams_of[3], (KNOTS, KNOTS), KNOTS ** -0.5, 0.125, ((0, 8),), jnp.float32),
        "neighbours": draw_neighbours(jax.random.fold_in(streams_of[6], 71), 0),
        "counts": draw_counts(jax.random.fold_in(streams_of[6], 71), 0),
    }


COV_RANGE = 0.05
TAPER_LEN = 0.15
KNOT_REACH = 0.15
TAPER_SCALE = 0.1
PROJ_GAIN = 0.5
EXPAND_GAIN = 0.5
LOW_SCALE = 0.5
NUGGET = 0.25
PRECISE = lax.Precision.HIGHEST

def tapered(own_locs, near_locs, near_vals, weights):
    delta_x = own_locs[0][:, None, :, None] - near_locs[0][:, :, None, :]
    delta_y = own_locs[1][:, None, :, None] - near_locs[1][:, :, None, :]
    distance = jnp.sqrt(delta_x * delta_x + delta_y * delta_y)
    scaled = jnp.minimum(distance / TAPER_LEN, 1.0)
    remain = (1.0 - scaled) * (1.0 - scaled)
    kernel = jnp.exp(-distance / COV_RANGE) * remain * remain * (1.0 + 4.0 * scaled) * weights[:, :, None, None]
    return jnp.einsum('gkpq,rgkq->rgp', kernel, near_vals, precision=PRECISE)

def knot_kernel(points, knot_pts, knot_range):
    delta_x = points[0][:, None] - knot_pts[0][None, :]
    delta_y = points[1][:, None] - knot_pts[1][None, :]
    return jnp.exp(-jnp.sqrt(delta_x * delta_x + delta_y * delta_y) / knot_range)

def reference(probes, locations, knot_locs, knot_precision, neighbours, counts):
    groups = NB // NBD
    row_count = NBD * BLOCK
    knot_range = KNOT_REACH * math.sqrt(NB / KNOTS)
    loc_blocks = locations.reshape(2, NB, BLOCK)
    val_blocks = probes.reshape(PROBES, NB, BLOCK)
    slot_ids = jnp.arange(KNB, dtype=jnp.int32)

    def one_group(group_index):
        first_block = group_index * NBD
        block_ids = lax.dynamic_slice_in_dim(neighbours, first_block, NBD, 0)
        live_count = lax.dynamic_slice_in_dim(counts, first_block, NBD, 0)
        weights = (slot_ids[None, :] < live_count[:, None]).astype(jnp.float32)
        own_locs = lax.dynamic_slice_in_dim(loc_blocks, first_block, NBD, 1)
        return tapered(own_locs, loc_blocks[:, block_ids], val_blocks[:, block_ids], weights)
    taper_part = lax.map(one_group, jnp.arange(groups, dtype=jnp.int32))
    taper_part = jnp.transpose(taper_part, (1, 0, 2, 3)).reshape(PROBES, NOBS)
    loc_rows = jnp.transpose(locations.reshape(2, groups, row_count), (1, 0, 2))
    val_rows = jnp.transpose(probes.reshape(PROBES, groups, row_count), (1, 0, 2))

    def accumulate(running, row_pair):
        kernel = knot_kernel(row_pair[0], knot_locs, knot_range)
        return (running + jnp.dot(row_pair[1], kernel, precision=PRECISE), None)
    projection, _ = lax.scan(accumulate, jnp.zeros((PROBES, KNOTS), jnp.float32), (loc_rows, val_rows))
    projection = projection * (PROJ_GAIN * math.sqrt(KNOTS / NOBS))
    factor = lax.dot_general(projection, knot_precision, (((1,), (1,)), ((), ())), precision=PRECISE)

    def expand(points):
        return lax.dot_general(factor, knot_kernel(points, knot_locs, knot_range), (((1,), (1,)), ((), ())), precision=PRECISE)
    low_part = lax.map(expand, loc_rows)
    low_part = jnp.transpose(low_part, (1, 0, 2)).reshape(PROBES, NOBS)
    low_part = low_part * EXPAND_GAIN
    return TAPER_SCALE * taper_part + LOW_SCALE * low_part + NUGGET * probes
```

```python
import functools
import math

import jax
import jax.numpy as jnp
from jax import lax
from jax.experimental import pallas as pl
from jax.experimental.pallas import tpu as pltpu
from jax.sharding import PartitionSpec as P

COV_RANGE = 0.05
TAPER_LEN = 0.15
KNOT_REACH = 0.15
TAPER_SCALE = 0.1
PROJ_GAIN = 0.5
EXPAND_GAIN = 0.5
LOW_SCALE = 0.5
NUGGET = 0.25
TINY = 1e-30

NX = 4
CELL = 128
F32 = jnp.float32
BF16 = jnp.bfloat16
NT = (((1,), (1,)), ((), ()))


def split(v):
    hi = v.astype(BF16)
    return hi, (v - hi.astype(F32)).astype(BF16)


def dist(ax, ay, bx, by):
    dx = ax - bx
    dy = ay - by
    q = dx * dx + dy * dy
    return q * lax.rsqrt(jnp.maximum(q, TINY))


def body(
    cfg,
    probes,
    locs,
    knots,
    prec,
    nbr,
    cnt,
    out,
    near,
    kl,
    oax,
    oay,
    obx,
    oby,
    pv,
    wv,
    khi,
    klo,
    pf,
    phi,
    plo,
    rs_src,
    rs_dst,
    zb,
    pj,
    fb,
    ct_hi,
    ct_lo,
    vals,
    tap,
    low,
    p_sem,
    kl_s,
    kl_r,
    h_s,
    h_r,
    rs_s,
    rs_r,
    z_s,
    z_r,
    g_s,
    g_r,
    f_s,
    f_r,
    relay,
):
    ns, nk, nz, nb, alpha, beta = cfg
    rows = nb * CELL
    s = lax.axis_index("space")
    k = lax.axis_index("knot")
    x = s // nz
    z = s % nz

    def space_at(dx, dz):
        return ((x + dx) % NX) * nz + (z + dz) % nz

    def knot_at(i):
        return (k + i) % nk

    def copy(src, dst, ss, rr, sp, kn):
        return pltpu.make_async_remote_copy(
            src_ref=src,
            dst_ref=dst,
            send_sem=ss,
            recv_sem=rr,
            device_id={"space": sp, "knot": kn},
            device_id_type=pl.DeviceIdType.MESH,
        )

    def tell(sem, sp, kn):
        pl.semaphore_signal(
            sem,
            inc=1,
            device_id={"space": sp, "knot": kn},
            device_id_type=pl.DeviceIdType.MESH,
        )

    mid = (CELL, rows)
    first, last = (CELL, CELL), (rows, CELL)
    below, above = (0, CELL), (rows + CELL, CELL)
    halo = []
    for ds in (1, -1):
        col = 1 - ds
        halo.append((ds, 0, mid, col, mid))
        halo.append((ds, 1, last, col, below))
        halo.append((ds, -1, first, col, above))
    halo.append((0, 1, last, 1, below))
    halo.append((0, -1, first, 1, above))

    barrier = pltpu.get_barrier_semaphore()
    count = 0
    for ds, dk, _, _, _ in halo[:6]:
        tell(barrier, (s + ds + ns) % ns, knot_at(dk + nk))
        count += 1
    for dz in (1, nz - 1):
        tell(barrier, space_at(0, dz), k)
        count += 1

    @pl.loop(1, NX * nk)
    def _(j):
        tell(barrier, space_at(j % NX, 0), knot_at(j // NX))

    count += NX * nk - 1

    p_copy = pltpu.make_async_copy(prec, pf, p_sem)
    p_copy.start()

    near[1, 0:16, CELL : CELL + rows] = probes[...]
    near[1, 16:24, CELL : CELL + rows] = jnp.zeros((8, rows), F32)
    near[1, 16:18, CELL : CELL + rows] = locs[...] * beta
    kl[0] = jnp.zeros((8, CELL), F32)
    for h in range(2):
        kl[0, h : h + 1, :] = knots[0:1, h * CELL : (h + 1) * CELL] * alpha
        kl[0, 2 + h : 3 + h, :] = knots[1:2, h * CELL : (h + 1) * CELL] * alpha
    p_hi, p_lo = split(probes[...])
    pv[0:16, :] = p_hi
    pv[16:32, :] = p_lo

    @pl.loop(0, nb)
    def _(b):
        at = pl.multiple_of(b * CELL, CELL)
        cx = jnp.broadcast_to(locs[0:1, pl.ds(at, CELL)], (CELL, CELL)).T
        cy = jnp.broadcast_to(locs[1:2, pl.ds(at, CELL)], (CELL, CELL)).T
        oax[pl.ds(at, CELL), :] = cx * alpha
        oay[pl.ds(at, CELL), :] = cy * alpha
        obx[pl.ds(at, CELL), :] = cx * beta
        oby[pl.ds(at, CELL), :] = cy * beta

    slot = lax.broadcasted_iota(jnp.int32, (nb, nb), 1)
    row = lax.broadcasted_iota(jnp.int32, (nb, nb), 0)
    live = jnp.zeros((nb, nb), jnp.int32)
    for b in range(nb):
        live = jnp.where(row == b, cnt[b], live)
    ids = nbr[...]
    own = s * (nk * nb) + k * nb + row
    for c in range(3):
        for j in range(3):
            hit = (ids == own + (c - 1) * (nk * nb) + (j - 1)) & (slot < live)
            w = jnp.sum(jnp.where(hit, 1.0, 0.0), axis=1, keepdims=True)
            wv[c * 3 + j] = jnp.broadcast_to(w, (nb, CELL))

    def group(i):
        base = pl.multiple_of(i * 2 * CELL, 2 * CELL)

        @pl.loop(0, nb)
        def _(b):
            at = pl.multiple_of(b * CELL, CELL)
            ax = oax[pl.ds(at, CELL), :]
            ay = oay[pl.ds(at, CELL), :]
            for h in range(2):
                d = dist(ax, ay, kl[i, h : h + 1, :], kl[i, 2 + h : 3 + h, :])
                hi, lo = split(jnp.exp(-d))
                lanes = pl.ds(pl.multiple_of(base + h * CELL, CELL), CELL)
                khi[pl.ds(at, CELL), lanes] = hi
                klo[pl.ds(at, CELL), lanes] = lo

        lanes = pl.ds(base, 2 * CELL)
        r = jnp.dot(pv[...], khi[:, lanes], preferred_element_type=F32)
        r2 = jnp.dot(pv[0:16, :], klo[:, lanes], preferred_element_type=F32)
        proj = r[0:16] + r[16:32] + r2
        for t in range(4):
            a, h = t // 2, t % 2
            rs_src[i, t] = proj[8 * a : 8 * a + 8, CELL * h : CELL * h + CELL]

    def rs_copy(i, dx):
        return copy(
            rs_src.at[i, (x + dx) % NX],
            rs_dst.at[i, dx],
            rs_s.at[i, dx],
            rs_r.at[i, dx],
            space_at(dx, 0),
            knot_at(i),
        )

    group(0)
    pl.semaphore_wait(barrier, count)

    kl_copies = [
        copy(kl.at[0], kl.at[i], kl_s.at[i], kl_r.at[i], s, knot_at(nk - i))
        for i in range(1, nk)
    ]
    for c in kl_copies:
        c.start()
    h_copies = []
    for n, (ds, dk, (a, w), col, (ta, tw)) in enumerate(halo):
        h_copies.append(
            copy(
                near.at[1, :, pl.ds(a, w)],
                near.at[col, :, pl.ds(ta, tw)],
                h_s.at[n],
                h_r.at[n],
                (s + ds + ns) % ns,
                knot_at(dk + nk),
            )
        )
    for c in h_copies:
        c.start()
    for dx in range(1, NX):
        rs_copy(0, dx).start()

    def groups(lo, hi):
        @pl.loop(lo, hi)
        def _(i):
            copy(
                kl.at[0], kl.at[i], kl_s.at[i], kl_r.at[i], s, knot_at(nk - i)
            ).wait_recv()
            group(i)
            for dx in range(NX):
                rs_copy(i, dx).start()

    def relay_tell(r):
        d = 2**r
        for dz in (d, nz - d):
            tell(relay.at[r], space_at(0, dz), k)

    def relay_wait(r):
        pl.semaphore_wait(relay.at[r], 2)

    relay_tell(0)
    groups(1, 4)
    relay_wait(0)
    relay_tell(1)
    groups(4, 6)
    relay_wait(1)
    relay_tell(2)
    groups(6, nk)

    def taper(lo_b, hi_b):
        @pl.loop(lo_b, hi_b)
        def _(b):
            at = pl.multiple_of(b * CELL, CELL)
            bx = obx[pl.ds(at, CELL), :]
            by = oby[pl.ds(at, CELL), :]
            for c in range(3):
                for j in range(3):
                    n = c * 3 + j
                    lanes = pl.ds(pl.multiple_of(at + j * CELL, CELL), CELL)
                    d = dist(bx, by, near[c, 16:17, lanes], near[c, 17:18, lanes])
                    rest = 1.0 - jnp.minimum(d, 1.0)
                    r2 = rest * rest
                    v = jnp.exp(d * (-TAPER_LEN / COV_RANGE))
                    v = v * (r2 * r2) * (5.0 - 4.0 * rest)
                    hi, lo = split(v)
                    ct_hi[:, n * CELL : (n + 1) * CELL] = hi
                    ct_lo[:, n * CELL : (n + 1) * CELL] = lo
                    m = near[c, 0:16, lanes] * wv[n, pl.ds(b, 1), :]
                    hi, lo = split(m)
                    vals[0:16, n * CELL : (n + 1) * CELL] = hi
                    vals[16:32, n * CELL : (n + 1) * CELL] = lo
            r = lax.dot_general(vals[...], ct_hi[...], NT, preferred_element_type=F32)
            r2 = lax.dot_general(
                vals[0:16, :], ct_lo[...], NT, preferred_element_type=F32
            )
            tap[:, pl.ds(at, CELL)] = r[0:16] + r[16:32] + r2

    for c in h_copies:
        c.wait_recv()
    taper(0, 3)

    @pl.loop(1, NX * nk)
    def _(j):
        rs_copy(j // NX, j % NX).wait_recv()

    total = rs_src[0, x]
    for j in range(1, NX * nk):
        total = total + rs_dst[j // NX, j % NX]
    zb[0] = total
    relay_wait(2)

    def z_copy(d):
        return copy(
            zb.at[0], zb.at[d], z_s.at[d], z_r.at[d], space_at(0, d), k
        )

    @pl.loop(1, nz)
    def _(d):
        z_copy(d).start()

    p_copy.wait()

    @pl.loop(0, nk)
    def _(i):
        lanes = pl.ds(pl.multiple_of(i * 2 * CELL, 2 * CELL), 2 * CELL)
        hi, lo = split(pf[:, lanes])
        phi[:, lanes] = hi
        plo[:, lanes] = lo

    taper(3, nb)

    @pl.loop(1, nz)
    def _(d):
        z_copy(d).wait_recv()

    total = zb[0]
    for d in range(1, nz):
        total = total + zb[d]
    pj[0, x] = total

    def g_copy(i, dx):
        return copy(
            pj.at[0, x],
            pj.at[i, x],
            g_s.at[i, dx],
            g_r.at[i, dx],
            space_at(dx, 0),
            knot_at(i),
        )

    def g_arrival(i, dx):
        return copy(
            pj.at[0, x],
            pj.at[i, (x + NX - dx) % NX],
            g_s.at[i, dx],
            g_r.at[i, dx],
            space_at(dx, 0),
            knot_at(i),
        )

    @pl.loop(1, NX * nk)
    def _(j):
        g_copy(j // NX, j % NX).start()

    @pl.loop(1, NX * nk)
    def _(j):
        g_arrival(j // NX, j % NX).wait_recv()

    fac = jnp.zeros((16, 2 * CELL), F32)
    for i in range(nk):
        g = knot_at(nk - i)
        lanes = pl.ds(pl.multiple_of(g * 2 * CELL, 2 * CELL), 2 * CELL)
        top = jnp.concatenate([pj[i, 0], pj[i, 1]], axis=1)
        bottom = jnp.concatenate([pj[i, 2], pj[i, 3]], axis=1)
        hi, lo = split(jnp.concatenate([top, bottom], axis=0))
        both = jnp.concatenate([hi, lo], axis=0)
        r = lax.dot_general(both, phi[:, lanes], NT, preferred_element_type=F32)
        r2 = lax.dot_general(hi, plo[:, lanes], NT, preferred_element_type=F32)
        fac = fac + (r[0:16] + r[16:32] + r2)
    fb[0] = fac

    def f_copy(i):
        return copy(fb.at[0], fb.at[i], f_s.at[i], f_r.at[i], s, knot_at(nk - i))

    for i in range(1, nk):
        f_copy(i).start()

    low[...] = jnp.zeros((16, rows), F32)

    @pl.loop(0, nk)
    def _(i):
        @pl.when(i > 0)
        def _():
            f_copy(i).wait_recv()

        lanes = pl.ds(pl.multiple_of(i * 2 * CELL, 2 * CELL), 2 * CELL)
        hi, lo = split(fb[i])
        both = jnp.concatenate([hi, lo], axis=0)
        r = lax.dot_general(both, khi[:, lanes], NT, preferred_element_type=F32)
        r2 = lax.dot_general(hi, klo[:, lanes], NT, preferred_element_type=F32)
        low[...] += r[0:16] + r[16:32] + r2

    coef = (
        LOW_SCALE
        * EXPAND_GAIN
        * PROJ_GAIN
        * math.sqrt(nk * 2 * CELL / (ns * nk * rows))
    )
    out[...] = TAPER_SCALE * tap[...] + coef * low[...]

    for c in kl_copies + h_copies:
        c.wait_send()

    @pl.loop(1, NX * nk)
    def _(j):
        rs_copy(j // NX, j % NX).wait_send()
        g_copy(j // NX, j % NX).wait_send()

    @pl.loop(1, nz)
    def _(d):
        z_copy(d).wait_send()

    for i in range(1, nk):
        f_copy(i).wait_send()


def shards(probes, locations, knot_locs, knot_precision, neighbours, counts):
    ns, nk = lax.axis_size("space"), lax.axis_size("knot")
    nz = ns // NX
    nb = neighbours.shape[0]
    rows = nb * CELL
    knots = knot_locs.shape[1]
    cols = knots * nk
    alpha = 1.0 / (KNOT_REACH * math.sqrt(nb * ns * nk / cols))
    beta = 1.0 / TAPER_LEN
    vmem = pl.BlockSpec(memory_space=pltpu.VMEM)
    dma = pltpu.SemaphoreType.DMA
    low = pl.pallas_call(
        functools.partial(body, (ns, nk, nz, nb, alpha, beta)),
        out_shape=jax.ShapeDtypeStruct(probes.shape, F32),
        in_specs=[
            vmem,
            vmem,
            vmem,
            pl.BlockSpec(memory_space=pl.ANY),
            vmem,
            pl.BlockSpec(memory_space=pltpu.SMEM),
        ],
        out_specs=vmem,
        scratch_shapes=[
            pltpu.VMEM((3, 24, rows + 2 * CELL), F32),
            pltpu.VMEM((nk, 8, CELL), F32),
            pltpu.VMEM((rows, CELL), F32),
            pltpu.VMEM((rows, CELL), F32),
            pltpu.VMEM((rows, CELL), F32),
            pltpu.VMEM((rows, CELL), F32),
            pltpu.VMEM((32, rows), BF16),
            pltpu.VMEM((9, nb, CELL), F32),
            pltpu.VMEM((rows, cols), BF16),
            pltpu.VMEM((rows, cols), BF16),
            pltpu.VMEM((knots, cols), F32),
            pltpu.VMEM((knots, cols), BF16),
            pltpu.VMEM((knots, cols), BF16),
            pltpu.VMEM((nk, 4, 8, CELL), F32),
            pltpu.VMEM((nk, 4, 8, CELL), F32),
            pltpu.VMEM((nz, 8, CELL), F32),
            pltpu.VMEM((nk, 4, 8, CELL), F32),
            pltpu.VMEM((nk, 16, 2 * CELL), F32),
            pltpu.VMEM((CELL, 9 * CELL), BF16),
            pltpu.VMEM((CELL, 9 * CELL), BF16),
            pltpu.VMEM((32, 9 * CELL), BF16),
            pltpu.VMEM((16, rows), F32),
            pltpu.VMEM((16, rows), F32),
            dma,
            dma((nk,)),
            dma((nk,)),
            dma((8,)),
            dma((8,)),
            dma((nk, NX)),
            dma((nk, NX)),
            dma((nz,)),
            dma((nz,)),
            dma((nk, NX)),
            dma((nk, NX)),
            dma((nk,)),
            dma((nk,)),
            pltpu.SemaphoreType.REGULAR((3,)),
        ],
        compiler_params=pltpu.CompilerParams(
            collective_id=0, has_side_effects=True, vmem_limit_bytes=48 << 20
        ),
    )(probes, locations, knot_locs, knot_precision, neighbours, counts)
    return low + NUGGET * probes


def solution(mesh):
    return jax.shard_map(
        shards,
        mesh=mesh,
        in_specs=(
            P(None, ("space", "knot")),
            P(None, ("space", "knot")),
            P(None, "knot"),
            P("knot", None),
            P(("space", "knot"), None),
            P(("space", "knot")),
        ),
        out_specs=P(None, ("space", "knot")),
        check_vma=False,
    )
```

```python
import functools
import math

import jax
import jax.numpy as jnp
from jax import lax
from jax.experimental import pallas as pl
from jax.experimental.pallas import tpu as pltpu
from jax.sharding import PartitionSpec as P

COV_RANGE = 0.05
TAPER_LEN = 0.15
KNOT_REACH = 0.15
TAPER_SCALE = 0.1
PROJ_GAIN = 0.5
EXPAND_GAIN = 0.5
LOW_SCALE = 0.5
NUGGET = 0.25
TINY = 1e-30
LOG2E = 1.0 / math.log(2.0)

NX = 4
NY = 4
CELL = 128
F32 = jnp.float32
BF16 = jnp.bfloat16
NT = (((1,), (1,)), ((), ()))
ORDER = ((0, 0), (0, 1), (1, 0), (3, 0), (2, 0), (2, 1), (1, 1), (3, 1))
STEP = tuple((-dy % NY, dc) for dy, dc in ORDER)
BACK = tuple(ORDER.index(st) for st in STEP)
NK = len(ORDER)
ARRIVE = (0, 1, 2, 3, 6, 7, 4, 5)
PLACE = tuple(ARRIVE.index(n) for n in range(NK))


def split(v):
    hi = v.astype(BF16)
    return hi, (v - hi.astype(F32)).astype(BF16)


def dist(ax, ay, bx, by):
    dx = ax - bx
    dy = ay - by
    q = dx * dx + dy * dy
    return q * lax.rsqrt(jnp.maximum(q, TINY))


def body(
    cfg,
    probes_hbm,
    locs_hbm,
    knots_hbm,
    prec,
    nbr_hbm,
    cnt_hbm,
    out,
    probes,
    locs,
    knots,
    nbr,
    cnt,
    near,
    kl,
    oax,
    oay,
    obx,
    oby,
    pv,
    wv,
    kk,
    pacc,
    pf,
    phi,
    plo,
    rs_src,
    rs_dst,
    zb,
    pj,
    fb,
    ct_hi,
    ct_lo,
    vals,
    tap,
    low,
    in_s,
    kl_s,
    kl_r,
    h_s,
    h_r,
    rs_s,
    rs_r,
    z_s,
    z_r,
    g_s,
    g_r,
    f_s,
    f_r,
    relay,
):
    ns, nz, nb, alpha, beta = cfg
    rows = nb * CELL
    s = lax.axis_index("space")
    k = lax.axis_index("knot")
    x = s // nz
    z = s % nz
    y = k // 2
    core = k % 2

    xs = [x] + [(x + d) % NX for d in range(1, NX)]
    sp = [xx * nz + z for xx in xs]
    zp = [x * nz + (z + d) % nz for d in range(nz)]
    east = ((s + ns - 1) % ns, (s + 1) % ns)
    ys = [y] + [(y + d) % NY for d in range(1, NY)]
    kn = [ys[dy] * 2 + (core + dc) % 2 for dy, dc in ORDER]

    def copy(src, dst, ss, rr, to_s, to_k):
        return pltpu.make_async_remote_copy(
            src_ref=src,
            dst_ref=dst,
            send_sem=ss,
            recv_sem=rr,
            device_id={"space": to_s, "knot": to_k},
            device_id_type=pl.DeviceIdType.MESH,
        )

    def tell(sem, to_s, to_k):
        pl.semaphore_signal(
            sem,
            inc=1,
            device_id={"space": to_s, "knot": to_k},
            device_id_type=pl.DeviceIdType.MESH,
        )

    barrier = pltpu.get_barrier_semaphore()
    for n in range(1, NK):
        tell(barrier, s, kn[n])
    for d in range(1, NX):
        tell(barrier, sp[d], k)
    for to_s in east:
        tell(barrier, to_s, k)
    for d in (1, 2, nz - 1, nz - 2):
        tell(barrier, zp[d], k)
    greeted = NK - 1 + NX - 1 + 2 + 4

    pairs = (
        (knots_hbm, knots),
        (locs_hbm, locs),
        (probes_hbm, probes),
        (nbr_hbm, nbr),
        (cnt_hbm, cnt),
        (prec, pf),
    )
    loads = [pltpu.make_async_copy(a, b, in_s.at[n]) for n, (a, b) in enumerate(pairs)]
    for c in loads:
        c.start()

    kl[0] = jnp.zeros((8, CELL), F32)
    loads[0].wait()
    for h in range(2):
        kl[0, h : h + 1, :] = knots[0:1, h * CELL : (h + 1) * CELL] * alpha
        kl[0, 2 + h : 3 + h, :] = knots[1:2, h * CELL : (h + 1) * CELL] * alpha

    def project(n, at, width):
        lanes = pl.ds(at, width)
        rhs = jnp.concatenate([kk[4 * n + m, lanes, :] for m in range(4)], axis=1)
        return jnp.dot(pv[:, lanes], rhs, preferred_element_type=F32)

    def ship(n, r):
        w = 2 * CELL
        proj = r[0:16, 0:w] + r[16:32, 0:w] + (r[0:16, w:] + r[16:32, w:])
        for t in range(NX):
            for h in range(2):
                rs_src[n * NX + t, 4 * h : 4 * h + 4] = proj[
                    4 * t : 4 * t + 4, CELL * h : CELL * h + CELL
                ]

    def group(n, prev):
        wide = 2 * CELL

        @pl.loop(0, rows // wide)
        def _(b):
            at = pl.multiple_of(b * wide, wide)
            if prev is not None:
                pacc[...] += project(prev, at, wide)
            for u in range(2):
                part = pl.ds(pl.multiple_of(at + u * CELL, CELL), CELL)
                ax = oax[part, :]
                ay = oay[part, :]
                for h in range(2):
                    d = dist(ax, ay, kl[n, h : h + 1, :], kl[n, 2 + h : 3 + h, :])
                    hi, lo = split(jnp.exp2(-d))
                    kk[4 * n + h, part, :] = hi
                    kk[4 * n + 2 + h, part, :] = lo

        if prev is not None:
            ship(prev, pacc[...])
        pacc[...] = jnp.zeros((32, 4 * CELL), F32)

    def rs_copy(n, d):
        return copy(
            rs_src.at[n * NX + xs[d]],
            rs_dst.at[n * NX + d],
            rs_s,
            rs_r,
            sp[d],
            kn[n],
        )

    def rs_start(n):
        for d in range(0 if n else 1, NX):
            rs_copy(n, d).start()

    def kl_copy(n):
        return copy(
            kl.at[0], kl.at[BACK[n]], kl_s, kl_r.at[BACK[n]], s, kn[n]
        )

    def kl_arrival(n):
        return copy(kl.at[0], kl.at[n], kl_s, kl_r.at[n], s, kn[n])

    pl.semaphore_wait(barrier, greeted)

    for n in range(1, NK):
        kl_copy(n).start()
    for d in range(1, NX):
        tell(relay.at[0], sp[d], k)
    for to_s in east:
        tell(relay.at[0], to_s, k)
    for d in (2, nz - 2):
        tell(relay.at[0], zp[d], k)

    near[1, 16:24, CELL : CELL + rows] = jnp.zeros((8, rows), F32)
    loads[1].wait()
    near[1, 16:18, CELL : CELL + rows] = locs[...] * beta
    @pl.loop(0, nb)
    def _(b):
        at = pl.multiple_of(b * CELL, CELL)
        cx = jnp.broadcast_to(locs[0:1, pl.ds(at, CELL)], (CELL, CELL)).T
        cy = jnp.broadcast_to(locs[1:2, pl.ds(at, CELL)], (CELL, CELL)).T
        oax[pl.ds(at, CELL), :] = cx * alpha
        oay[pl.ds(at, CELL), :] = cy * alpha
        obx[pl.ds(at, CELL), :] = cx * beta
        oby[pl.ds(at, CELL), :] = cy * beta

    loads[2].wait()
    near[1, 0:16, CELL : CELL + rows] = probes[...]
    p_hi, p_lo = split(probes[...])
    pv[0:16, :] = p_hi
    pv[16:32, :] = p_lo
    group(0, None)

    mid = (CELL, rows)
    first, last = (CELL, CELL), (rows, CELL)
    below, above = (0, CELL), (rows + CELL, CELL)
    up, down = (k + 1) % NK, (k + NK - 1) % NK
    halo = [
        (east[1], k, mid, 0, mid),
        (east[0], k, mid, 2, mid),
        (s, up, last, 1, below),
        (s, down, first, 1, above),
        (east[1], up, last, 0, below),
        (east[1], down, first, 0, above),
        (east[0], up, last, 2, below),
        (east[0], down, first, 2, above),
    ]
    h_copies = [
        copy(
            near.at[1, :, pl.ds(a, w)],
            near.at[col, :, pl.ds(ta, tw)],
            h_s.at[0 if n < 2 else 1],
            h_r.at[(0, 2, 1, 3, 0, 0, 2, 2)[n]],
            to_s,
            to_k,
        )
        for n, (to_s, to_k, (a, w), col, (ta, tw)) in enumerate(halo)
    ]
    for c in h_copies[:4]:
        c.start()

    kl_arrival(1).wait_recv()
    group(1, 0)
    kl_arrival(2).wait_recv()
    group(2, 1)
    pl.semaphore_wait(relay.at[0], NX - 1 + 2 + 2)
    for d in (4, nz - 4):
        tell(relay.at[1], zp[d], k)
    for c in h_copies[4:]:
        c.start()
    rs_start(0)
    rs_start(1)
    for n in range(3, NK):
        kl_arrival(n).wait_recv()
        group(n, n - 1)
        rs_start(n - 1)
    ship(NK - 1, project(NK - 1, 0, rows))
    rs_start(NK - 1)

    slot = lax.broadcasted_iota(jnp.int32, (nb, nb), 1)
    row = lax.broadcasted_iota(jnp.int32, (nb, nb), 0)
    loads[3].wait()
    loads[4].wait()
    live = jnp.zeros((nb, nb), jnp.int32)
    for b in range(nb):
        live = jnp.where(row == b, cnt[b], live)
    ids = nbr[...]
    own = s * (NK * nb) + k * nb + row
    for c in range(3):
        for j in range(3):
            hit = (ids == own + (c - 1) * (NK * nb) + (j - 1)) & (slot < live)
            w = jnp.sum(jnp.where(hit, 1.0, 0.0), axis=1, keepdims=True)
            wv[c * 3 + j] = jnp.broadcast_to(w, (nb, CELL))

    def taper(lo_b, hi_b):
        @pl.loop(lo_b, hi_b)
        def _(b):
            at = pl.multiple_of(b * CELL, CELL)
            bx = obx[pl.ds(at, CELL), :]
            by = oby[pl.ds(at, CELL), :]
            for c in range(3):
                for j in range(3):
                    n = c * 3 + j
                    lanes = pl.ds(pl.multiple_of(at + j * CELL, CELL), CELL)
                    d = dist(bx, by, near[c, 16:17, lanes], near[c, 17:18, lanes])
                    rest = 1.0 - jnp.minimum(d, 1.0)
                    r2 = rest * rest
                    v = jnp.exp2(d * (-TAPER_LEN / COV_RANGE * LOG2E))
                    v = v * (r2 * r2) * (5.0 - 4.0 * rest)
                    hi, lo = split(v)
                    ct_hi[n] = hi
                    ct_lo[n] = lo
                    m = near[c, 0:16, lanes] * wv[n, pl.ds(b, 1), :]
                    hi, lo = split(m)
                    vals[0:16, n * CELL : (n + 1) * CELL] = hi
                    vals[16:32, n * CELL : (n + 1) * CELL] = lo
            c_hi = jnp.concatenate([ct_hi[n] for n in range(9)], axis=1)
            c_lo = jnp.concatenate([ct_lo[n] for n in range(9)], axis=1)
            r = lax.dot_general(vals[...], c_hi, NT, preferred_element_type=F32)
            r2 = lax.dot_general(vals[0:16, :], c_lo, NT, preferred_element_type=F32)
            tap[:, pl.ds(at, CELL)] = r[0:16] + r[16:32] + r2

    def bulk(src, dst, ss, rr):
        return copy(src, dst, ss, rr, s, kn[1])

    bulk(near.at[0], near.at[0], h_s.at[0], h_r.at[0]).wait_recv()
    bulk(near.at[2], near.at[2], h_s.at[0], h_r.at[2]).wait_recv()
    h_copies[2].wait_recv()
    h_copies[3].wait_recv()
    taper(0, 3)
    others = [(n, d) for n in range(NK) for d in range(NX) if n or d]
    rest_of = pl.ds(1, NK * NX - 1)
    bulk(rs_src.at[rest_of], rs_dst.at[rest_of], rs_s, rs_r).wait_recv()

    total = rs_src[x]
    for n, d in others:
        total = total + rs_dst[n * NX + d]
    zb[0] = total
    pl.semaphore_wait(relay.at[1], 2)

    def z_copy(d):
        return copy(zb.at[0], zb.at[d], z_s, z_r, zp[d], k)

    for d in sorted(range(1, nz), key=lambda d: -min(d, nz - d)):
        z_copy(d).start()

    loads[5].wait()

    @pl.loop(0, NK)
    def _(i):
        lanes = pl.ds(pl.multiple_of(i * 2 * CELL, 2 * CELL), 2 * CELL)
        hi, lo = split(pf[:, lanes])
        phi[:, lanes] = hi
        plo[:, lanes] = lo

    taper(3, nb)
    low[...] = jnp.zeros((16, rows), F32)
    bulk(kl.at[pl.ds(1, NK - 1)], kl.at[pl.ds(1, NK - 1)], kl_s, kl_r.at[0]).wait_send()
    some = near.at[pl.ds(0, 2), :, pl.ds(CELL, rows)]
    bulk(some, some, h_s.at[0], h_r.at[0]).wait_send()
    some = near.at[:, :, pl.ds(0, 2 * CELL)]
    bulk(some, some, h_s.at[1], h_r.at[0]).wait_send()
    bulk(rs_src.at[rest_of], rs_dst.at[rest_of], rs_s, rs_r).wait_send()
    others_z = zb.at[pl.ds(1, nz - 1)]
    bulk(others_z, others_z, z_s, z_r).wait_recv()
    total = zb[0]
    for d in range(1, nz):
        total = total + zb[d]
    pj[0] = total

    def g_copy(n):
        return copy(
            pj.at[0], pj.at[BACK[n]], g_s, g_r.at[BACK[n]], s, kn[n]
        )

    def g_arrival(n):
        return copy(pj.at[0], pj.at[n], g_s, g_r.at[n], s, kn[n])

    for n in (4, 5, 2, 3, 6, 7, 1):
        g_copy(n).start()
    bulk(others_z, others_z, z_s, z_r).wait_send()
    fac = jnp.zeros((4, 2 * CELL), F32)
    for n in ARRIVE:
        if n:
            g_arrival(n).wait_recv()
        lanes = pl.ds(pl.multiple_of(kn[n] * 2 * CELL, 2 * CELL), 2 * CELL)
        piece = pj[n]
        hi, lo = split(jnp.concatenate([piece[0:4], piece[4:8]], axis=1))
        both = jnp.concatenate([hi.astype(F32), lo.astype(F32)], axis=0).astype(BF16)
        r = lax.dot_general(both, phi[:, lanes], NT, preferred_element_type=F32)
        r2 = lax.dot_general(both, plo[:, lanes], NT, preferred_element_type=F32)
        fac = fac + ((r[0:4] + r[4:8]) + (r2[0:4] + r2[4:8]))
    fb[x, 0:4] = fac[:, 0:CELL]
    fb[x, 4:8] = fac[:, CELL:]

    def f_copy(n, d):
        m = BACK[n]
        return copy(
            fb.at[x], fb.at[m * NX + x], f_s, f_r.at[PLACE[m] // 2], sp[d], kn[n]
        )

    for n in (4, 5, 2, 3, 6, 7, 1, 0):
        for d in (2, 1, 3, 0):
            if n or d:
                f_copy(n, d).start()
    bulk(pj.at[pl.ds(1, NK - 1)], pj.at[pl.ds(1, NK - 1)], g_s, g_r.at[0]).wait_send()

    def expand(slots):
        cols, hi_slabs, lo_slabs = [], [], []
        for n in slots:
            for h in range(2):
                part = [fb[n * NX + t, 4 * h : 4 * h + 4] for t in range(NX)]
                cols.append(jnp.concatenate(part, axis=0))
                hi_slabs.append(4 * n + h)
                lo_slabs.append(4 * n + 2 + h)
        hi, lo = split(jnp.concatenate(cols, axis=1))
        both = jnp.concatenate([hi, lo], axis=0)
        k_hi = jnp.concatenate([kk[m] for m in hi_slabs], axis=1)
        k_lo = jnp.concatenate([kk[m] for m in lo_slabs], axis=1)
        r = lax.dot_general(both, k_hi, NT, preferred_element_type=F32)
        r2 = lax.dot_general(hi, k_lo, NT, preferred_element_type=F32)
        low[...] += r[0:16] + r[16:32] + r2

    for m in range(4):
        slots = ARRIVE[2 * m : 2 * m + 2]
        first_piece = max(slots[0] * NX, 1)
        part = fb.at[pl.ds(first_piece, (slots[0] + 2) * NX - first_piece)]
        bulk(part, part, f_s, f_r.at[m]).wait_recv()
        expand(slots)

    coef = (
        LOW_SCALE
        * EXPAND_GAIN
        * PROJ_GAIN
        * math.sqrt(NK * 2 * CELL / (ns * NK * rows))
    )

    rest = fb.at[pl.ds(1, NK * NX - 1)]
    bulk(rest, rest, f_s, f_r.at[0]).wait_send()
    out[...] = TAPER_SCALE * tap[...] + coef * low[...] + NUGGET * probes[...]


def shards(probes, locations, knot_locs, knot_precision, neighbours, counts):
    ns = lax.axis_size("space")
    nz = ns // NX
    nb = neighbours.shape[0]
    rows = nb * CELL
    knots = knot_locs.shape[1]
    cols = knots * NK
    alpha = LOG2E / (KNOT_REACH * math.sqrt(nb * ns * NK / cols))
    beta = 1.0 / TAPER_LEN
    dma = pltpu.SemaphoreType.DMA
    applied = pl.pallas_call(
        functools.partial(body, (ns, nz, nb, alpha, beta)),
        out_shape=jax.ShapeDtypeStruct(probes.shape, F32),
        in_specs=[pl.BlockSpec(memory_space=pltpu.HBM)] * 6,
        out_specs=pl.BlockSpec(memory_space=pltpu.VMEM),
        scratch_shapes=[
            pltpu.VMEM((16, rows), F32),
            pltpu.VMEM((2, rows), F32),
            pltpu.VMEM((2, knots), F32),
            pltpu.VMEM((nb, nb), jnp.int32),
            pltpu.SMEM((nb,), jnp.int32),
            pltpu.VMEM((3, 24, rows + 2 * CELL), F32),
            pltpu.VMEM((NK, 8, CELL), F32),
            pltpu.VMEM((rows, CELL), F32),
            pltpu.VMEM((rows, CELL), F32),
            pltpu.VMEM((rows, CELL), F32),
            pltpu.VMEM((rows, CELL), F32),
            pltpu.VMEM((32, rows), BF16),
            pltpu.VMEM((9, nb, CELL), F32),
            pltpu.VMEM((4 * NK, rows, CELL), BF16),
            pltpu.VMEM((32, 4 * CELL), F32),
            pltpu.VMEM((knots, cols), F32),
            pltpu.VMEM((knots, cols), BF16),
            pltpu.VMEM((knots, cols), BF16),
            pltpu.VMEM((NK * NX, 8, CELL), F32),
            pltpu.VMEM((NK * NX, 8, CELL), F32),
            pltpu.VMEM((nz, 8, CELL), F32),
            pltpu.VMEM((NK, 8, CELL), F32),
            pltpu.VMEM((NK * NX, 8, CELL), F32),
            pltpu.VMEM((9, CELL, CELL), BF16),
            pltpu.VMEM((9, CELL, CELL), BF16),
            pltpu.VMEM((32, 9 * CELL), BF16),
            pltpu.VMEM((16, rows), F32),
            pltpu.VMEM((16, rows), F32),
            dma((6,)),
            dma,
            dma((NK,)),
            dma((2,)),
            dma((4,)),
            dma,
            dma,
            dma,
            dma,
            dma,
            dma((NK,)),
            dma,
            dma((4,)),
            pltpu.SemaphoreType.REGULAR((2,)),
        ],
        compiler_params=pltpu.CompilerParams(
            collective_id=0, has_side_effects=True, vmem_limit_bytes=67043328
        ),
    )(probes, locations, knot_locs, knot_precision, neighbours, counts)
    return applied


def solution(mesh):
    return jax.shard_map(
        shards,
        mesh=mesh,
        in_specs=(
            P(None, ("space", "knot")),
            P(None, ("space", "knot")),
            P(None, "knot"),
            P("knot", None),
            P(("space", "knot"), None),
            P(("space", "knot")),
        ),
        out_specs=P(None, ("space", "knot")),
        check_vma=False,
    )
```

```python
import functools
import math

import jax
import jax.numpy as jnp
from jax import lax
from jax.experimental import pallas as pl
from jax.experimental.pallas import tpu as pltpu
from jax.sharding import PartitionSpec as P

COV_RANGE = 0.05
TAPER_LEN = 0.15
KNOT_REACH = 0.15
TAPER_SCALE = 0.1
PROJ_GAIN = 0.5
EXPAND_GAIN = 0.5
LOW_SCALE = 0.5
NUGGET = 0.25
TINY = 1e-30
LOG2E = 1.0 / math.log(2.0)

NX = 4
NY = 4
CELL = 128
F32 = jnp.float32
BF16 = jnp.bfloat16
NT = (((1,), (1,)), ((), ()))
ORDER = ((0, 0), (0, 1), (1, 0), (3, 0), (2, 0), (2, 1), (1, 1), (3, 1))
STEP = tuple((-dy % NY, dc) for dy, dc in ORDER)
BACK = tuple(ORDER.index(st) for st in STEP)
NK = len(ORDER)
ARRIVE = (0, 1, 2, 3, 6, 7, 4, 5)
PLACE = tuple(ARRIVE.index(n) for n in range(NK))


def split(v):
    hi = v.astype(BF16)
    return hi, (v - hi.astype(F32)).astype(BF16)


def dist(ax, ay, bx, by):
    dx = ax - bx
    dy = ay - by
    q = dx * dx + dy * dy
    return q * lax.rsqrt(jnp.maximum(q, TINY))


def body(
    cfg,
    probes_hbm,
    locs_hbm,
    knots_hbm,
    prec,
    nbr_hbm,
    cnt_hbm,
    out,
    probes,
    locs,
    knots,
    nbr,
    cnt,
    near,
    kl,
    oax,
    oay,
    obx,
    oby,
    pv,
    wv,
    kk,
    pacc,
    pf,
    phi,
    plo,
    rs_src,
    rs_dst,
    zb,
    pj,
    fb,
    ct_hi,
    ct_lo,
    vals,
    tap,
    low,
    in_s,
    kl_s,
    kl_r,
    h_s,
    h_r,
    rs_s,
    rs_r,
    z_s,
    z_r,
    g_s,
    g_r,
    f_s,
    f_r,
    relay,
):
    ns, nz, nb, alpha, beta = cfg
    rows = nb * CELL
    s = lax.axis_index("space")
    k = lax.axis_index("knot")
    x = s // nz
    z = s % nz
    y = k // 2
    core = k % 2

    xs = [x] + [(x + d) % NX for d in range(1, NX)]
    sp = [xx * nz + z for xx in xs]
    zp = [x * nz + (z + d) % nz for d in range(nz)]
    east = ((s + ns - 1) % ns, (s + 1) % ns)
    ys = [y] + [(y + d) % NY for d in range(1, NY)]
    kn = [ys[dy] * 2 + (core + dc) % 2 for dy, dc in ORDER]

    def copy(src, dst, ss, rr, to_s, to_k):
        return pltpu.make_async_remote_copy(
            src_ref=src,
            dst_ref=dst,
            send_sem=ss,
            recv_sem=rr,
            device_id={"space": to_s, "knot": to_k},
            device_id_type=pl.DeviceIdType.MESH,
        )

    def tell(sem, to_s, to_k):
        pl.semaphore_signal(
            sem,
            inc=1,
            device_id={"space": to_s, "knot": to_k},
            device_id_type=pl.DeviceIdType.MESH,
        )

    barrier = pltpu.get_barrier_semaphore()
    for n in range(1, NK):
        tell(barrier, s, kn[n])
    for d in range(1, NX):
        tell(barrier, sp[d], k)
    for to_s in east:
        tell(barrier, to_s, k)
    for d in (1, 2, nz - 1, nz - 2):
        tell(barrier, zp[d], k)
    greeted = NK - 1 + NX - 1 + 2 + 4

    pairs = (
        (knots_hbm, knots),
        (locs_hbm, locs),
        (probes_hbm, probes),
        (nbr_hbm, nbr),
        (cnt_hbm, cnt),
        (prec, pf),
    )
    loads = [pltpu.make_async_copy(a, b, in_s.at[n]) for n, (a, b) in enumerate(pairs)]
    for c in loads:
        c.start()

    kl[0] = jnp.zeros((8, CELL), F32)
    loads[0].wait()
    for h in range(2):
        kl[0, h : h + 1, :] = knots[0:1, h * CELL : (h + 1) * CELL] * alpha
        kl[0, 2 + h : 3 + h, :] = knots[1:2, h * CELL : (h + 1) * CELL] * alpha

    def project(n, at, width):
        lanes = pl.ds(at, width)
        rhs = jnp.concatenate([kk[4 * n + m, lanes, :] for m in range(4)], axis=1)
        return jnp.dot(pv[:, lanes], rhs, preferred_element_type=F32)

    def ship(n, r):
        w = 2 * CELL
        proj = r[0:16, 0:w] + r[16:32, 0:w] + (r[0:16, w:] + r[16:32, w:])
        for t in range(NX):
            for h in range(2):
                rs_src[n * NX + t, 4 * h : 4 * h + 4] = proj[
                    4 * t : 4 * t + 4, CELL * h : CELL * h + CELL
                ]

    def group(n, prev):
        if prev is not None:
            r = project(prev, 0, rows)
        for b in range(nb):
            part = slice(b * CELL, (b + 1) * CELL)
            ax = oax[part, :]
            ay = oay[part, :]
            for h in range(2):
                d = dist(ax, ay, kl[n, h : h + 1, :], kl[n, 2 + h : 3 + h, :])
                hi, lo = split(jnp.exp2(-d))
                kk[4 * n + h, part, :] = hi
                kk[4 * n + 2 + h, part, :] = lo
        if prev is not None:
            ship(prev, r)

    def rs_copy(n, d):
        return copy(
            rs_src.at[n * NX + xs[d]],
            rs_dst.at[n * NX + d],
            rs_s,
            rs_r,
            sp[d],
            kn[n],
        )

    def rs_start(n):
        for d in range(0 if n else 1, NX):
            rs_copy(n, d).start()

    def kl_copy(n):
        return copy(
            kl.at[0], kl.at[BACK[n]], kl_s, kl_r.at[BACK[n]], s, kn[n]
        )

    def kl_arrival(n):
        return copy(kl.at[0], kl.at[n], kl_s, kl_r.at[n], s, kn[n])

    near[1, 16:24, CELL : CELL + rows] = jnp.zeros((8, rows), F32)
    loads[1].wait()
    near[1, 16:18, CELL : CELL + rows] = locs[...] * beta
    @pl.loop(0, nb)
    def _(b):
        at = pl.multiple_of(b * CELL, CELL)
        cx = jnp.broadcast_to(locs[0:1, pl.ds(at, CELL)], (CELL, CELL)).T
        cy = jnp.broadcast_to(locs[1:2, pl.ds(at, CELL)], (CELL, CELL)).T
        oax[pl.ds(at, CELL), :] = cx * alpha
        oay[pl.ds(at, CELL), :] = cy * alpha
        obx[pl.ds(at, CELL), :] = cx * beta
        oby[pl.ds(at, CELL), :] = cy * beta

    loads[2].wait()
    near[1, 0:16, CELL : CELL + rows] = probes[...]
    p_hi, p_lo = split(probes[...])
    pv[0:16, :] = p_hi
    pv[16:32, :] = p_lo
    pl.semaphore_wait(barrier, greeted)

    for n in range(1, NK):
        kl_copy(n).start()
    for d in range(1, NX):
        tell(relay.at[0], sp[d], k)
    for to_s in east:
        tell(relay.at[0], to_s, k)
    for d in (2, nz - 2):
        tell(relay.at[0], zp[d], k)

    group(0, None)

    mid = (CELL, rows)
    first, last = (CELL, CELL), (rows, CELL)
    below, above = (0, CELL), (rows + CELL, CELL)
    up, down = (k + 1) % NK, (k + NK - 1) % NK
    halo = [
        (east[1], k, mid, 0, mid),
        (east[0], k, mid, 2, mid),
        (s, up, last, 1, below),
        (s, down, first, 1, above),
        (east[1], up, last, 0, below),
        (east[1], down, first, 0, above),
        (east[0], up, last, 2, below),
        (east[0], down, first, 2, above),
    ]
    h_copies = [
        copy(
            near.at[1, :, pl.ds(a, w)],
            near.at[col, :, pl.ds(ta, tw)],
            h_s.at[0 if n < 2 else 1],
            h_r.at[(0, 2, 1, 3, 0, 0, 2, 2)[n]],
            to_s,
            to_k,
        )
        for n, (to_s, to_k, (a, w), col, (ta, tw)) in enumerate(halo)
    ]
    for c in h_copies[:4]:
        c.start()

    kl_arrival(1).wait_recv()
    group(1, 0)
    kl_arrival(2).wait_recv()
    group(2, 1)
    pl.semaphore_wait(relay.at[0], NX - 1 + 2 + 2)
    for d in (4, nz - 4):
        tell(relay.at[1], zp[d], k)
    for c in h_copies[4:]:
        c.start()
    rs_start(0)
    rs_start(1)
    for n in range(3, NK):
        kl_arrival(n).wait_recv()
        group(n, n - 1)
        rs_start(n - 1)
    ship(NK - 1, project(NK - 1, 0, rows))
    rs_start(NK - 1)

    slot = lax.broadcasted_iota(jnp.int32, (nb, nb), 1)
    row = lax.broadcasted_iota(jnp.int32, (nb, nb), 0)
    loads[3].wait()
    loads[4].wait()
    live = jnp.zeros((nb, nb), jnp.int32)
    for b in range(nb):
        live = jnp.where(row == b, cnt[b], live)
    ids = nbr[...]
    own = s * (NK * nb) + k * nb + row
    for c in range(3):
        for j in range(3):
            hit = (ids == own + (c - 1) * (NK * nb) + (j - 1)) & (slot < live)
            w = jnp.sum(jnp.where(hit, 1.0, 0.0), axis=1, keepdims=True)
            wv[c * 3 + j] = jnp.broadcast_to(w, (nb, CELL))

    def taper(lo_b, hi_b):
        @pl.loop(lo_b, hi_b)
        def _(b):
            at = pl.multiple_of(b * CELL, CELL)
            bx = obx[pl.ds(at, CELL), :]
            by = oby[pl.ds(at, CELL), :]
            for c in range(3):
                for j in range(3):
                    n = c * 3 + j
                    lanes = pl.ds(pl.multiple_of(at + j * CELL, CELL), CELL)
                    d = dist(bx, by, near[c, 16:17, lanes], near[c, 17:18, lanes])
                    rest = 1.0 - jnp.minimum(d, 1.0)
                    r2 = rest * rest
                    v = jnp.exp2(d * (-TAPER_LEN / COV_RANGE * LOG2E))
                    v = v * (r2 * r2) * (5.0 - 4.0 * rest)
                    hi, lo = split(v)
                    ct_hi[n] = hi
                    ct_lo[n] = lo
                    m = near[c, 0:16, lanes] * wv[n, pl.ds(b, 1), :]
                    hi, lo = split(m)
                    vals[0:16, n * CELL : (n + 1) * CELL] = hi
                    vals[16:32, n * CELL : (n + 1) * CELL] = lo
            c_hi = jnp.concatenate([ct_hi[n] for n in range(9)], axis=1)
            c_lo = jnp.concatenate([ct_lo[n] for n in range(9)], axis=1)
            r = lax.dot_general(vals[...], c_hi, NT, preferred_element_type=F32)
            r2 = lax.dot_general(vals[0:16, :], c_lo, NT, preferred_element_type=F32)
            tap[:, pl.ds(at, CELL)] = r[0:16] + r[16:32] + r2

    def bulk(src, dst, ss, rr):
        return copy(src, dst, ss, rr, s, kn[1])

    bulk(near.at[0], near.at[0], h_s.at[0], h_r.at[0]).wait_recv()
    bulk(near.at[2], near.at[2], h_s.at[0], h_r.at[2]).wait_recv()
    h_copies[2].wait_recv()
    h_copies[3].wait_recv()
    taper(0, 3)
    others = [(n, d) for n in range(NK) for d in range(NX) if n or d]
    rest_of = pl.ds(1, NK * NX - 1)
    bulk(rs_src.at[rest_of], rs_dst.at[rest_of], rs_s, rs_r).wait_recv()

    total = rs_src[x]
    for n, d in others:
        total = total + rs_dst[n * NX + d]
    zb[0] = total
    pl.semaphore_wait(relay.at[1], 2)

    def z_copy(d):
        return copy(zb.at[0], zb.at[d], z_s, z_r, zp[d], k)

    for d in sorted(range(1, nz), key=lambda d: -min(d, nz - d)):
        z_copy(d).start()

    loads[5].wait()

    @pl.loop(0, NK)
    def _(i):
        lanes = pl.ds(pl.multiple_of(i * 2 * CELL, 2 * CELL), 2 * CELL)
        hi, lo = split(pf[:, lanes])
        phi[:, lanes] = hi
        plo[:, lanes] = lo

    taper(3, nb)
    low[...] = jnp.zeros((16, rows), F32)
    bulk(kl.at[pl.ds(1, NK - 1)], kl.at[pl.ds(1, NK - 1)], kl_s, kl_r.at[0]).wait_send()
    some = near.at[pl.ds(0, 2), :, pl.ds(CELL, rows)]
    bulk(some, some, h_s.at[0], h_r.at[0]).wait_send()
    some = near.at[:, :, pl.ds(0, 2 * CELL)]
    bulk(some, some, h_s.at[1], h_r.at[0]).wait_send()
    bulk(rs_src.at[rest_of], rs_dst.at[rest_of], rs_s, rs_r).wait_send()
    others_z = zb.at[pl.ds(1, nz - 1)]
    bulk(others_z, others_z, z_s, z_r).wait_recv()
    total = zb[0]
    for d in range(1, nz):
        total = total + zb[d]
    pj[0] = total

    def g_copy(n):
        return copy(
            pj.at[0], pj.at[BACK[n]], g_s, g_r.at[BACK[n]], s, kn[n]
        )

    def g_arrival(n):
        return copy(pj.at[0], pj.at[n], g_s, g_r.at[n], s, kn[n])

    for n in (4, 5, 2, 3, 6, 7, 1):
        g_copy(n).start()
    bulk(others_z, others_z, z_s, z_r).wait_send()
    fac = jnp.zeros((4, 2 * CELL), F32)
    for n in ARRIVE:
        if n:
            g_arrival(n).wait_recv()
        lanes = pl.ds(pl.multiple_of(kn[n] * 2 * CELL, 2 * CELL), 2 * CELL)
        piece = pj[n]
        hi, lo = split(jnp.concatenate([piece[0:4], piece[4:8]], axis=1))
        both = jnp.concatenate([hi.astype(F32), lo.astype(F32)], axis=0).astype(BF16)
        r = lax.dot_general(both, phi[:, lanes], NT, preferred_element_type=F32)
        r2 = lax.dot_general(both, plo[:, lanes], NT, preferred_element_type=F32)
        fac = fac + ((r[0:4] + r[4:8]) + (r2[0:4] + r2[4:8]))
    fb[x, 0:4] = fac[:, 0:CELL]
    fb[x, 4:8] = fac[:, CELL:]

    def f_copy(n, d):
        m = BACK[n]
        return copy(
            fb.at[x], fb.at[m * NX + x], f_s, f_r.at[PLACE[m] // 2], sp[d], kn[n]
        )

    for n in (0, 1, 3, 2, 7, 6, 4, 5):
        for d in (2, 1, 3, 0):
            if n or d:
                f_copy(n, d).start()
    bulk(pj.at[pl.ds(1, NK - 1)], pj.at[pl.ds(1, NK - 1)], g_s, g_r.at[0]).wait_send()

    def expand(slots):
        cols, hi_slabs, lo_slabs = [], [], []
        for n in slots:
            for h in range(2):
                part = [fb[n * NX + t, 4 * h : 4 * h + 4] for t in range(NX)]
                cols.append(jnp.concatenate(part, axis=0))
                hi_slabs.append(4 * n + h)
                lo_slabs.append(4 * n + 2 + h)
        hi, lo = split(jnp.concatenate(cols, axis=1))
        both = jnp.concatenate([hi, lo], axis=0)
        k_hi = jnp.concatenate([kk[m] for m in hi_slabs], axis=1)
        k_lo = jnp.concatenate([kk[m] for m in lo_slabs], axis=1)
        r = lax.dot_general(both, k_hi, NT, preferred_element_type=F32)
        r2 = lax.dot_general(hi, k_lo, NT, preferred_element_type=F32)
        low[...] += r[0:16] + r[16:32] + r2

    for m in range(4):
        slots = ARRIVE[2 * m : 2 * m + 2]
        first_piece = max(slots[0] * NX, 1)
        part = fb.at[pl.ds(first_piece, (slots[0] + 2) * NX - first_piece)]
        bulk(part, part, f_s, f_r.at[m]).wait_recv()
        expand(slots)

    coef = (
        LOW_SCALE
        * EXPAND_GAIN
        * PROJ_GAIN
        * math.sqrt(NK * 2 * CELL / (ns * NK * rows))
    )

    rest = fb.at[pl.ds(1, NK * NX - 1)]
    bulk(rest, rest, f_s, f_r.at[0]).wait_send()
    out[...] = TAPER_SCALE * tap[...] + coef * low[...] + NUGGET * probes[...]


def shards(probes, locations, knot_locs, knot_precision, neighbours, counts):
    ns = lax.axis_size("space")
    nz = ns // NX
    nb = neighbours.shape[0]
    rows = nb * CELL
    knots = knot_locs.shape[1]
    cols = knots * NK
    alpha = LOG2E / (KNOT_REACH * math.sqrt(nb * ns * NK / cols))
    beta = 1.0 / TAPER_LEN
    dma = pltpu.SemaphoreType.DMA
    applied = pl.pallas_call(
        functools.partial(body, (ns, nz, nb, alpha, beta)),
        out_shape=jax.ShapeDtypeStruct(probes.shape, F32),
        in_specs=[pl.BlockSpec(memory_space=pltpu.HBM)] * 6,
        out_specs=pl.BlockSpec(memory_space=pltpu.VMEM),
        scratch_shapes=[
            pltpu.VMEM((16, rows), F32),
            pltpu.VMEM((2, rows), F32),
            pltpu.VMEM((2, knots), F32),
            pltpu.VMEM((nb, nb), jnp.int32),
            pltpu.SMEM((nb,), jnp.int32),
            pltpu.VMEM((3, 24, rows + 2 * CELL), F32),
            pltpu.VMEM((NK, 8, CELL), F32),
            pltpu.VMEM((rows, CELL), F32),
            pltpu.VMEM((rows, CELL), F32),
            pltpu.VMEM((rows, CELL), F32),
            pltpu.VMEM((rows, CELL), F32),
            pltpu.VMEM((32, rows), BF16),
            pltpu.VMEM((9, nb, CELL), F32),
            pltpu.VMEM((4 * NK, rows, CELL), BF16),
            pltpu.VMEM((32, 4 * CELL), F32),
            pltpu.VMEM((knots, cols), F32),
            pltpu.VMEM((knots, cols), BF16),
            pltpu.VMEM((knots, cols), BF16),
            pltpu.VMEM((NK * NX, 8, CELL), F32),
            pltpu.VMEM((NK * NX, 8, CELL), F32),
            pltpu.VMEM((nz, 8, CELL), F32),
            pltpu.VMEM((NK, 8, CELL), F32),
            pltpu.VMEM((NK * NX, 8, CELL), F32),
            pltpu.VMEM((9, CELL, CELL), BF16),
            pltpu.VMEM((9, CELL, CELL), BF16),
            pltpu.VMEM((32, 9 * CELL), BF16),
            pltpu.VMEM((16, rows), F32),
            pltpu.VMEM((16, rows), F32),
            dma((6,)),
            dma,
            dma((NK,)),
            dma((2,)),
            dma((4,)),
            dma,
            dma,
            dma,
            dma,
            dma,
            dma((NK,)),
            dma,
            dma((4,)),
            pltpu.SemaphoreType.REGULAR((2,)),
        ],
        compiler_params=pltpu.CompilerParams(
            collective_id=0, has_side_effects=True, vmem_limit_bytes=48 << 20
        ),
    )(*(pltpu.with_memory_space_constraint(a, pltpu.HBM) for a in (probes, locations, knot_locs, knot_precision, neighbours, counts)))
    return applied


def solution(mesh):
    return jax.shard_map(
        shards,
        mesh=mesh,
        in_specs=(
            P(None, ("space", "knot")),
            P(None, ("space", "knot")),
            P(None, "knot"),
            P("knot", None),
            P(("space", "knot"), None),
            P(("space", "knot")),
        ),
        out_specs=P(None, ("space", "knot")),
        check_vma=False,
    )
```

```python
import functools
import math

import jax
import jax.numpy as jnp
from jax import lax
from jax.experimental import pallas as pl
from jax.experimental.pallas import tpu as pltpu
from jax.sharding import PartitionSpec as P

COV_RANGE = 0.05
TAPER_LEN = 0.15
KNOT_REACH = 0.15
TAPER_SCALE = 0.1
PROJ_GAIN = 0.5
EXPAND_GAIN = 0.5
LOW_SCALE = 0.5
NUGGET = 0.25
TINY = 1e-30
LOG2E = 1.0 / math.log(2.0)

NX = 4
NY = 4
CELL = 128
F32 = jnp.float32
BF16 = jnp.bfloat16
NT = (((1,), (1,)), ((), ()))
ORDER = ((0, 0), (0, 1), (3, 0), (1, 0), (2, 0), (2, 1), (1, 1), (3, 1))
STEP = tuple((-dy % NY, dc) for dy, dc in ORDER)
BACK = tuple(ORDER.index(st) for st in STEP)
NK = len(ORDER)
ARRIVE = (0, 1, 2, 7, 3, 6, 4, 5)


def split(v):
    hi = v.astype(BF16)
    return hi, (v - hi.astype(F32)).astype(BF16)


def dist(ax, ay, bx, by):
    dx = ax - bx
    dy = ay - by
    q = dx * dx + dy * dy
    return q * lax.rsqrt(jnp.maximum(q, TINY))


def body(
    cfg,
    probes_hbm,
    locs_hbm,
    knots_hbm,
    prec,
    nbr_hbm,
    cnt_hbm,
    out,
    probes,
    locs,
    knots,
    nbr,
    cnt,
    near,
    kl,
    oax,
    oay,
    obx,
    oby,
    pv,
    wv,
    kk,
    pacc,
    pf,
    phi,
    plo,
    rs_src,
    rs_dst,
    zb,
    pj,
    fb,
    ct_hi,
    ct_lo,
    vals,
    tap,
    low,
    in_s,
    kl_s,
    kl_r,
    h_s,
    h_r,
    rs_s,
    rs_r,
    z_s,
    z_r,
    g_s,
    g_r,
    f_s,
    f_r,
    relay,
):
    ns, nz, nb, alpha, beta = cfg
    rows = nb * CELL
    s = lax.axis_index("space")
    k = lax.axis_index("knot")
    x = s // nz
    z = s % nz
    y = k // 2
    core = k % 2

    xs = [x] + [(x + d) % NX for d in range(1, NX)]
    sp = [xx * nz + z for xx in xs]
    zp = [x * nz + (z + d) % nz for d in range(nz)]
    east = ((s + ns - 1) % ns, (s + 1) % ns)
    ys = [y] + [(y + d) % NY for d in range(1, NY)]
    kn = [ys[dy] * 2 + (core + dc) % 2 for dy, dc in ORDER]

    def copy(src, dst, ss, rr, to_s, to_k):
        return pltpu.make_async_remote_copy(
            src_ref=src,
            dst_ref=dst,
            send_sem=ss,
            recv_sem=rr,
            device_id={"space": to_s, "knot": to_k},
            device_id_type=pl.DeviceIdType.MESH,
        )

    def tell(sem, to_s, to_k):
        pl.semaphore_signal(
            sem,
            inc=1,
            device_id={"space": to_s, "knot": to_k},
            device_id_type=pl.DeviceIdType.MESH,
        )

    barrier = pltpu.get_barrier_semaphore()
    for n in range(1, NK):
        tell(barrier, s, kn[n])
    for d in range(1, NX):
        tell(barrier, sp[d], k)
    for to_s in east:
        tell(barrier, to_s, k)
    for d in (1, 2, nz - 1, nz - 2):
        tell(barrier, zp[d], k)
    greeted = NK - 1 + NX - 1 + 2 + 4

    pairs = (
        (knots_hbm, knots),
        (locs_hbm, locs),
        (probes_hbm, probes),
        (nbr_hbm, nbr),
        (cnt_hbm, cnt),
        (prec, pf),
    )
    loads = [pltpu.make_async_copy(a, b, in_s.at[n]) for n, (a, b) in enumerate(pairs)]
    for c in loads:
        c.start()

    kl[0] = jnp.zeros((8, CELL), F32)
    loads[0].wait()
    for h in range(2):
        kl[0, h : h + 1, :] = knots[0:1, h * CELL : (h + 1) * CELL] * alpha
        kl[0, 2 + h : 3 + h, :] = knots[1:2, h * CELL : (h + 1) * CELL] * alpha

    def project(n, at, width):
        lanes = pl.ds(at, width)
        rhs = jnp.concatenate([kk[4 * n + m, lanes, :] for m in range(4)], axis=1)
        return jnp.dot(pv[:, lanes], rhs, preferred_element_type=F32)

    def ship(n, r):
        w = 2 * CELL
        proj = r[0:16, 0:w] + r[16:32, 0:w] + (r[0:16, w:] + r[16:32, w:])
        for t in range(NX):
            for h in range(2):
                rs_src[n * NX + t, 4 * h : 4 * h + 4] = proj[
                    4 * t : 4 * t + 4, CELL * h : CELL * h + CELL
                ]

    def group(n, prev):
        if prev is not None:
            r = project(prev, 0, rows)
        for b in range(nb):
            if n == NK - 1 and b == nb // 2:
                pacc[...] = project(n, 0, rows // 2)
            part = slice(b * CELL, (b + 1) * CELL)
            ax = oax[part, :]
            ay = oay[part, :]
            for h in range(2):
                d = dist(ax, ay, kl[n, h : h + 1, :], kl[n, 2 + h : 3 + h, :])
                hi, lo = split(jnp.exp2(-d))
                kk[4 * n + h, part, :] = hi
                kk[4 * n + 2 + h, part, :] = lo
        if prev is not None:
            ship(prev, r)

    def rs_copy(n, d):
        return copy(
            rs_src.at[n * NX + xs[d]],
            rs_dst.at[n * NX + d],
            rs_s,
            rs_r,
            sp[d],
            kn[n],
        )

    def rs_start(n):
        for d in (2, 1, 3, 0) if n else (2, 1, 3):
            rs_copy(n, d).start()

    def kl_copy(n):
        return copy(
            kl.at[0], kl.at[BACK[n]], kl_s, kl_r.at[BACK[n]], s, kn[n]
        )

    def kl_arrival(n):
        return copy(kl.at[0], kl.at[n], kl_s, kl_r.at[n], s, kn[n])

    near[1, 16:24, CELL : CELL + rows] = jnp.zeros((8, rows), F32)
    loads[1].wait()
    near[1, 16:18, CELL : CELL + rows] = locs[...] * beta
    @pl.loop(0, nb // 2)
    def _(b):
        for u in range(2):
            at = pl.ds(pl.multiple_of(b * 2 * CELL + u * CELL, CELL), CELL)
            cx = jnp.broadcast_to(locs[0:1, at], (CELL, CELL)).T
            cy = jnp.broadcast_to(locs[1:2, at], (CELL, CELL)).T
            oax[at, :] = cx * alpha
            oay[at, :] = cy * alpha
            obx[at, :] = cx * beta
            oby[at, :] = cy * beta

    loads[2].wait()
    near[1, 0:16, CELL : CELL + rows] = probes[...]
    p_hi, p_lo = split(probes[...])
    pv[0:16, :] = p_hi
    pv[16:32, :] = p_lo
    pl.semaphore_wait(barrier, greeted)

    for n in range(1, NK):
        kl_copy(n).start()
    for d in range(1, NX):
        tell(relay.at[0], sp[d], k)
    for to_s in east:
        tell(relay.at[0], to_s, k)
    for d in (2, nz - 2):
        tell(relay.at[0], zp[d], k)

    group(0, None)

    mid = (CELL, rows)
    first, last = (CELL, CELL), (rows, CELL)
    below, above = (0, CELL), (rows + CELL, CELL)
    up, down = (k + 1) % NK, (k + NK - 1) % NK
    halo = [
        (east[1], k, mid, 0, mid),
        (east[0], k, mid, 2, mid),
        (s, up, last, 1, below),
        (s, down, first, 1, above),
        (east[1], up, last, 0, below),
        (east[1], down, first, 0, above),
        (east[0], up, last, 2, below),
        (east[0], down, first, 2, above),
    ]
    h_copies = [
        copy(
            near.at[1, :, pl.ds(a, w)],
            near.at[col, :, pl.ds(ta, tw)],
            h_s.at[0 if n < 2 else 1],
            h_r.at[(0, 2, 1, 3, 0, 0, 2, 2)[n]],
            to_s,
            to_k,
        )
        for n, (to_s, to_k, (a, w), col, (ta, tw)) in enumerate(halo)
    ]
    for c in h_copies[:4]:
        c.start()

    kl_arrival(1).wait_recv()
    group(1, 0)
    kl_arrival(2).wait_recv()
    group(2, 1)
    pl.semaphore_wait(relay.at[0], NX - 1 + 2 + 2)
    for d in (4, nz - 4):
        tell(relay.at[1], zp[d], k)
    for c in h_copies[4:]:
        c.start()
    rs_start(0)
    rs_start(1)
    for n in range(3, NK):
        kl_arrival(n).wait_recv()
        group(n, n - 1)
        rs_start(n - 1)
    ship(NK - 1, pacc[...] + project(NK - 1, rows // 2, rows // 2))
    rs_start(NK - 1)

    slot = lax.broadcasted_iota(jnp.int32, (nb, nb), 1)
    row = lax.broadcasted_iota(jnp.int32, (nb, nb), 0)
    loads[3].wait()
    loads[4].wait()
    live = jnp.zeros((nb, nb), jnp.int32)
    for b in range(nb):
        live = jnp.where(row == b, cnt[b], live)
    ids = nbr[...]
    own = s * (NK * nb) + k * nb + row
    for c in range(3):
        for j in range(3):
            hit = (ids == own + (c - 1) * (NK * nb) + (j - 1)) & (slot < live)
            w = jnp.sum(jnp.where(hit, 1.0, 0.0), axis=1, keepdims=True)
            wv[c * 3 + j] = jnp.broadcast_to(w, (nb, CELL))

    def taper(lo_b, hi_b):
        @pl.loop(lo_b, hi_b)
        def _(b):
            at = pl.multiple_of(b * CELL, CELL)
            bx = obx[pl.ds(at, CELL), :]
            by = oby[pl.ds(at, CELL), :]
            for c in range(3):
                for j in range(3):
                    n = c * 3 + j
                    lanes = pl.ds(pl.multiple_of(at + j * CELL, CELL), CELL)
                    d = dist(bx, by, near[c, 16:17, lanes], near[c, 17:18, lanes])
                    rest = 1.0 - jnp.minimum(d, 1.0)
                    r2 = rest * rest
                    v = jnp.exp2(d * (-TAPER_LEN / COV_RANGE * LOG2E))
                    v = v * (r2 * r2) * (5.0 - 4.0 * rest)
                    hi, lo = split(v)
                    ct_hi[n] = hi
                    ct_lo[n] = lo
                    m = near[c, 0:16, lanes] * wv[n, pl.ds(b, 1), :]
                    hi, lo = split(m)
                    vals[0:16, n * CELL : (n + 1) * CELL] = hi
                    vals[16:32, n * CELL : (n + 1) * CELL] = lo
            c_hi = jnp.concatenate([ct_hi[n] for n in range(9)], axis=1)
            c_lo = jnp.concatenate([ct_lo[n] for n in range(9)], axis=1)
            r = lax.dot_general(vals[...], c_hi, NT, preferred_element_type=F32)
            r2 = lax.dot_general(vals[0:16, :], c_lo, NT, preferred_element_type=F32)
            tap[:, pl.ds(at, CELL)] = r[0:16] + r[16:32] + r2

    def bulk(src, dst, ss, rr):
        return copy(src, dst, ss, rr, s, kn[1])

    bulk(near.at[0], near.at[0], h_s.at[0], h_r.at[0]).wait_recv()
    bulk(near.at[2], near.at[2], h_s.at[0], h_r.at[2]).wait_recv()
    h_copies[2].wait_recv()
    h_copies[3].wait_recv()
    taper(0, 3)
    others = [(n, d) for n in range(NK) for d in range(NX) if n or d]
    rest_of = pl.ds(1, NK * NX - 1)
    bulk(rs_src.at[rest_of], rs_dst.at[rest_of], rs_s, rs_r).wait_recv()

    def tree(terms):
        while len(terms) > 1:
            pairs = [a + b for a, b in zip(terms[::2], terms[1::2])]
            terms = pairs + terms[len(terms) & ~1 :]
        return terms[0]

    zb[0] = tree([rs_src[x]] + [rs_dst[n * NX + d] for n, d in others])
    pl.semaphore_wait(relay.at[1], 2)

    def z_copy(d):
        return copy(zb.at[0], zb.at[d], z_s, z_r, zp[d], k)

    for d in sorted(range(1, nz), key=lambda d: -min(d, nz - d)):
        z_copy(d).start()

    loads[5].wait()

    @pl.loop(0, NK)
    def _(i):
        lanes = pl.ds(pl.multiple_of(i * 2 * CELL, 2 * CELL), 2 * CELL)
        hi, lo = split(pf[:, lanes])
        phi[:, lanes] = hi
        plo[:, lanes] = lo

    taper(3, nb)
    low[...] = jnp.zeros((16, rows), F32)
    bulk(kl.at[pl.ds(1, NK - 1)], kl.at[pl.ds(1, NK - 1)], kl_s, kl_r.at[0]).wait_send()
    some = near.at[pl.ds(0, 2), :, pl.ds(CELL, rows)]
    bulk(some, some, h_s.at[0], h_r.at[0]).wait_send()
    some = near.at[:, :, pl.ds(0, 2 * CELL)]
    bulk(some, some, h_s.at[1], h_r.at[0]).wait_send()
    bulk(rs_src.at[rest_of], rs_dst.at[rest_of], rs_s, rs_r).wait_send()
    others_z = zb.at[pl.ds(1, nz - 1)]
    bulk(others_z, others_z, z_s, z_r).wait_recv()
    pj[0] = tree([zb[d] for d in range(nz)])

    def g_copy(n):
        return copy(
            pj.at[0], pj.at[BACK[n]], g_s, g_r.at[BACK[n]], s, kn[n]
        )

    def g_arrival(n):
        return copy(pj.at[0], pj.at[n], g_s, g_r.at[n], s, kn[n])

    for n in (4, 5, 2, 3, 6, 7, 1):
        g_copy(n).start()
    bulk(others_z, others_z, z_s, z_r).wait_send()
    fac = jnp.zeros((4, 2 * CELL), F32)
    for slots in (ARRIVE[:4], ARRIVE[4:]):
        for n in slots:
            if n:
                g_arrival(n).wait_recv()
        for n in slots:
            lanes = pl.ds(pl.multiple_of(kn[n] * 2 * CELL, 2 * CELL), 2 * CELL)
            piece = pj[n]
            hi, lo = split(jnp.concatenate([piece[0:4], piece[4:8]], axis=1))
            both = jnp.concatenate([hi.astype(F32), lo.astype(F32)], axis=0)
            both = both.astype(BF16)
            r = lax.dot_general(both, phi[:, lanes], NT, preferred_element_type=F32)
            r2 = lax.dot_general(both, plo[:, lanes], NT, preferred_element_type=F32)
            fac = fac + ((r[0:4] + r[4:8]) + (r2[0:4] + r2[4:8]))
    fb[x, 0:4] = fac[:, 0:CELL]
    fb[x, 4:8] = fac[:, CELL:]

    def f_copy(n, d):
        m = BACK[n]
        return copy(
            fb.at[x], fb.at[m * NX + x], f_s, f_r.at[m], sp[d], kn[n]
        )

    for n in tuple(BACK[m] for m in ARRIVE):
        for d in (2, 1, 3, 0):
            if n or d:
                f_copy(n, d).start()
    bulk(pj.at[pl.ds(1, NK - 1)], pj.at[pl.ds(1, NK - 1)], g_s, g_r.at[0]).wait_send()

    def expand(slots):
        cols, hi_slabs, lo_slabs = [], [], []
        for n in slots:
            for h in range(2):
                part = [fb[n * NX + t, 4 * h : 4 * h + 4] for t in range(NX)]
                cols.append(jnp.concatenate(part, axis=0))
                hi_slabs.append(4 * n + h)
                lo_slabs.append(4 * n + 2 + h)
        hi, lo = split(jnp.concatenate(cols, axis=1))
        both = jnp.concatenate([hi, lo], axis=0)
        k_hi = jnp.concatenate([kk[m] for m in hi_slabs], axis=1)
        k_lo = jnp.concatenate([kk[m] for m in lo_slabs], axis=1)
        r = lax.dot_general(both, k_hi, NT, preferred_element_type=F32)
        r2 = lax.dot_general(hi, k_lo, NT, preferred_element_type=F32)
        low[...] += r[0:16] + r[16:32] + r2

    for n in ARRIVE:
        first_piece = max(n * NX, 1)
        part = fb.at[pl.ds(first_piece, (n + 1) * NX - first_piece)]
        bulk(part, part, f_s, f_r.at[n]).wait_recv()
        expand((n,))

    coef = (
        LOW_SCALE
        * EXPAND_GAIN
        * PROJ_GAIN
        * math.sqrt(NK * 2 * CELL / (ns * NK * rows))
    )

    rest = fb.at[pl.ds(1, NK * NX - 1)]
    bulk(rest, rest, f_s, f_r.at[0]).wait_send()
    out[...] = TAPER_SCALE * tap[...] + coef * low[...] + NUGGET * probes[...]


def shards(probes, locations, knot_locs, knot_precision, neighbours, counts):
    ns = lax.axis_size("space")
    nz = ns // NX
    nb = neighbours.shape[0]
    rows = nb * CELL
    knots = knot_locs.shape[1]
    cols = knots * NK
    alpha = LOG2E / (KNOT_REACH * math.sqrt(nb * ns * NK / cols))
    beta = 1.0 / TAPER_LEN
    dma = pltpu.SemaphoreType.DMA
    applied = pl.pallas_call(
        functools.partial(body, (ns, nz, nb, alpha, beta)),
        out_shape=jax.ShapeDtypeStruct(probes.shape, F32),
        in_specs=[pl.BlockSpec(memory_space=pltpu.HBM)] * 6,
        out_specs=pl.BlockSpec(memory_space=pltpu.VMEM),
        scratch_shapes=[
            pltpu.VMEM((16, rows), F32),
            pltpu.VMEM((2, rows), F32),
            pltpu.VMEM((2, knots), F32),
            pltpu.VMEM((nb, nb), jnp.int32),
            pltpu.SMEM((nb,), jnp.int32),
            pltpu.VMEM((3, 24, rows + 2 * CELL), F32),
            pltpu.VMEM((NK, 8, CELL), F32),
            pltpu.VMEM((rows, CELL), F32),
            pltpu.VMEM((rows, CELL), F32),
            pltpu.VMEM((rows, CELL), F32),
            pltpu.VMEM((rows, CELL), F32),
            pltpu.VMEM((32, rows), BF16),
            pltpu.VMEM((9, nb, CELL), F32),
            pltpu.VMEM((4 * NK, rows, CELL), BF16),
            pltpu.VMEM((32, 4 * CELL), F32),
            pltpu.VMEM((knots, cols), F32),
            pltpu.VMEM((knots, cols), BF16),
            pltpu.VMEM((knots, cols), BF16),
            pltpu.VMEM((NK * NX, 8, CELL), F32),
            pltpu.VMEM((NK * NX, 8, CELL), F32),
            pltpu.VMEM((nz, 8, CELL), F32),
            pltpu.VMEM((NK, 8, CELL), F32),
            pltpu.VMEM((NK * NX, 8, CELL), F32),
            pltpu.VMEM((9, CELL, CELL), BF16),
            pltpu.VMEM((9, CELL, CELL), BF16),
            pltpu.VMEM((32, 9 * CELL), BF16),
            pltpu.VMEM((16, rows), F32),
            pltpu.VMEM((16, rows), F32),
            dma((6,)),
            dma,
            dma((NK,)),
            dma((2,)),
            dma((4,)),
            dma,
            dma,
            dma,
            dma,
            dma,
            dma((NK,)),
            dma,
            dma((NK,)),
            pltpu.SemaphoreType.REGULAR((2,)),
        ],
        compiler_params=pltpu.CompilerParams(
            collective_id=0, has_side_effects=True, vmem_limit_bytes=48 << 20
        ),
    )(*(pltpu.with_memory_space_constraint(a, pltpu.HBM) for a in (probes, locations, knot_locs, knot_precision, neighbours, counts)))
    return applied


def solution(mesh):
    return jax.shard_map(
        shards,
        mesh=mesh,
        in_specs=(
            P(None, ("space", "knot")),
            P(None, ("space", "knot")),
            P(None, "knot"),
            P("knot", None),
            P(("space", "knot"), None),
            P(("space", "knot")),
        ),
        out_specs=P(None, ("space", "knot")),
        check_vma=False,
    )
```

```python
import functools
import math

import jax
import jax.numpy as jnp
from jax import lax
from jax.experimental import pallas as pl
from jax.experimental.pallas import tpu as pltpu
from jax.sharding import PartitionSpec as P

COV_RANGE = 0.05
TAPER_LEN = 0.15
KNOT_REACH = 0.15
TAPER_SCALE = 0.1
PROJ_GAIN = 0.5
EXPAND_GAIN = 0.5
LOW_SCALE = 0.5
NUGGET = 0.25
TINY = 1e-30
LOG2E = 1.0 / math.log(2.0)

NX = 4
NY = 4
CELL = 128
F32 = jnp.float32
BF16 = jnp.bfloat16
NT = (((1,), (1,)), ((), ()))
ORDER = ((0, 0), (0, 1), (3, 1), (1, 1), (2, 1), (2, 0), (1, 0), (3, 0))
STEP = tuple((-dy % NY, dc) for dy, dc in ORDER)
BACK = tuple(ORDER.index(st) for st in STEP)
NK = len(ORDER)
ARRIVE = (0, 1, 7, 2, 6, 3, 5, 4)


def split(v):
    hi = v.astype(BF16)
    return hi, (v - hi.astype(F32)).astype(BF16)


def dist(ax, ay, bx, by):
    dx = ax - bx
    dy = ay - by
    q = dx * dx + dy * dy
    return q * lax.rsqrt(jnp.maximum(q, TINY))


def body(
    cfg,
    probes_hbm,
    locs_hbm,
    knots_hbm,
    prec,
    nbr_hbm,
    cnt_hbm,
    out,
    probes,
    locs,
    knots,
    nbr,
    cnt,
    near,
    kl,
    oax,
    oay,
    obx,
    oby,
    pv,
    wv,
    kk,
    pacc,
    pf,
    phi,
    plo,
    rs_src,
    rs_dst,
    zb,
    pj,
    fb,
    ct_hi,
    ct_lo,
    vals,
    tap,
    low,
    in_s,
    kl_s,
    kl_r,
    h_s,
    h_r,
    rs_s,
    rs_r,
    z_s,
    z_r,
    g_s,
    g_r,
    f_s,
    f_r,
    relay,
):
    ns, nz, nb, alpha, beta = cfg
    rows = nb * CELL
    s = lax.axis_index("space")
    k = lax.axis_index("knot")
    x = s // nz
    z = s % nz
    y = k // 2
    core = k % 2

    xs = [x] + [(x + d) % NX for d in range(1, NX)]
    sp = [xx * nz + z for xx in xs]
    zp = [x * nz + (z + d) % nz for d in range(nz)]
    east = ((s + ns - 1) % ns, (s + 1) % ns)
    ys = [y] + [(y + d) % NY for d in range(1, NY)]
    kn = [ys[dy] * 2 + (core + dc) % 2 for dy, dc in ORDER]

    def copy(src, dst, ss, rr, to_s, to_k):
        return pltpu.make_async_remote_copy(
            src_ref=src,
            dst_ref=dst,
            send_sem=ss,
            recv_sem=rr,
            device_id={"space": to_s, "knot": to_k},
            device_id_type=pl.DeviceIdType.MESH,
        )

    def tell(sem, to_s, to_k):
        pl.semaphore_signal(
            sem,
            inc=1,
            device_id={"space": to_s, "knot": to_k},
            device_id_type=pl.DeviceIdType.MESH,
        )

    barrier = pltpu.get_barrier_semaphore()
    for n in range(1, NK):
        tell(barrier, s, kn[n])
    for d in range(1, NX):
        tell(barrier, sp[d], k)
    for to_s in east:
        tell(barrier, to_s, k)
    for d in (1, 2, nz - 1, nz - 2):
        tell(barrier, zp[d], k)
    greeted = NK - 1 + NX - 1 + 2 + 4

    pairs = (
        (knots_hbm, knots),
        (locs_hbm, locs),
        (probes_hbm, probes),
        (nbr_hbm, nbr),
        (cnt_hbm, cnt),
        (prec, pf),
    )
    loads = [pltpu.make_async_copy(a, b, in_s.at[n]) for n, (a, b) in enumerate(pairs)]
    for c in loads:
        c.start()

    kl[0] = jnp.zeros((8, CELL), F32)
    loads[0].wait()
    for h in range(2):
        kl[0, h : h + 1, :] = knots[0:1, h * CELL : (h + 1) * CELL] * alpha
        kl[0, 2 + h : 3 + h, :] = knots[1:2, h * CELL : (h + 1) * CELL] * alpha

    def project(n, at, width):
        lanes = pl.ds(at, width)
        rhs = jnp.concatenate([kk[4 * n + m, lanes, :] for m in range(4)], axis=1)
        return jnp.dot(pv[:, lanes], rhs, preferred_element_type=F32)

    def ship(n, r):
        w = 2 * CELL
        proj = r[0:16, 0:w] + r[16:32, 0:w] + (r[0:16, w:] + r[16:32, w:])
        for t in range(NX):
            for h in range(2):
                rs_src[n * NX + t, 4 * h : 4 * h + 4] = proj[
                    4 * t : 4 * t + 4, CELL * h : CELL * h + CELL
                ]

    def group(n, prev):
        if prev is not None:
            r = project(prev, 0, rows)
        for b in range(nb):
            if n == NK - 1 and b == nb // 2:
                pacc[...] = project(n, 0, rows // 2)
            part = slice(b * CELL, (b + 1) * CELL)
            ax = oax[part, :]
            ay = oay[part, :]
            for h in range(2):
                d = dist(ax, ay, kl[n, h : h + 1, :], kl[n, 2 + h : 3 + h, :])
                hi, lo = split(jnp.exp2(-d))
                kk[4 * n + h, part, :] = hi
                kk[4 * n + 2 + h, part, :] = lo
        if prev is not None:
            ship(prev, r)

    def rs_copy(n, d):
        return copy(
            rs_src.at[n * NX + xs[d]],
            rs_dst.at[n * NX + d],
            rs_s,
            rs_r,
            sp[d],
            kn[n],
        )

    def rs_start(n):
        for d in (2, 1, 3, 0) if n else (2, 1, 3):
            rs_copy(n, d).start()

    def kl_copy(n):
        return copy(
            kl.at[0], kl.at[BACK[n]], kl_s, kl_r.at[BACK[n]], s, kn[n]
        )

    def kl_arrival(n):
        return copy(kl.at[0], kl.at[n], kl_s, kl_r.at[n], s, kn[n])

    near[1, 16:24, CELL : CELL + rows] = jnp.zeros((8, rows), F32)
    loads[1].wait()
    near[1, 16:18, CELL : CELL + rows] = locs[...] * beta
    @pl.loop(0, nb // 2)
    def _(b):
        for u in range(2):
            at = pl.ds(pl.multiple_of(b * 2 * CELL + u * CELL, CELL), CELL)
            cx = jnp.broadcast_to(locs[0:1, at], (CELL, CELL)).T
            cy = jnp.broadcast_to(locs[1:2, at], (CELL, CELL)).T
            oax[at, :] = cx * alpha
            oay[at, :] = cy * alpha
            obx[at, :] = cx * beta
            oby[at, :] = cy * beta

    loads[2].wait()
    near[1, 0:16, CELL : CELL + rows] = probes[...]
    p_hi, p_lo = split(probes[...])
    pv[0:16, :] = p_hi
    pv[16:32, :] = p_lo
    pl.semaphore_wait(barrier, greeted)

    for n in (7, 6, 2, 3, 1, 4, 5):
        kl_copy(n).start()
    for d in range(1, NX):
        tell(relay.at[0], sp[d], k)
    for to_s in east:
        tell(relay.at[0], to_s, k)
    for d in (2, nz - 2):
        tell(relay.at[0], zp[d], k)

    group(0, None)

    mid = (CELL, rows)
    first, last = (CELL, CELL), (rows, CELL)
    below, above = (0, CELL), (rows + CELL, CELL)
    up, down = (k + 1) % NK, (k + NK - 1) % NK
    halo = [
        (east[1], k, mid, 0, mid),
        (east[0], k, mid, 2, mid),
        (s, up, last, 1, below),
        (s, down, first, 1, above),
        (east[1], up, last, 0, below),
        (east[1], down, first, 0, above),
        (east[0], up, last, 2, below),
        (east[0], down, first, 2, above),
    ]
    h_copies = [
        copy(
            near.at[1, :, pl.ds(a, w)],
            near.at[col, :, pl.ds(ta, tw)],
            h_s.at[0 if n < 2 else 1],
            h_r.at[(0, 2, 1, 3, 0, 0, 2, 2)[n]],
            to_s,
            to_k,
        )
        for n, (to_s, to_k, (a, w), col, (ta, tw)) in enumerate(halo)
    ]
    for c in h_copies[:4]:
        c.start()

    kl_arrival(1).wait_recv()
    group(1, 0)
    kl_arrival(2).wait_recv()
    group(2, 1)
    pl.semaphore_wait(relay.at[0], NX - 1 + 2 + 2)
    for d in (4, nz - 4):
        tell(relay.at[1], zp[d], k)
    for c in h_copies[4:]:
        c.start()
    rs_start(0)
    rs_start(1)
    for n in range(3, NK):
        kl_arrival(n).wait_recv()
        group(n, n - 1)
        rs_start(n - 1)
    ship(NK - 1, pacc[...] + project(NK - 1, rows // 2, rows // 2))
    rs_start(NK - 1)

    slot = lax.broadcasted_iota(jnp.int32, (nb, nb), 1)
    row = lax.broadcasted_iota(jnp.int32, (nb, nb), 0)
    loads[3].wait()
    loads[4].wait()
    live = jnp.zeros((nb, nb), jnp.int32)
    for b in range(nb):
        live = jnp.where(row == b, cnt[b], live)
    ids = nbr[...]
    own = s * (NK * nb) + k * nb + row
    for c in range(3):
        for j in range(3):
            hit = (ids == own + (c - 1) * (NK * nb) + (j - 1)) & (slot < live)
            w = jnp.sum(jnp.where(hit, 1.0, 0.0), axis=1, keepdims=True)
            wv[c * 3 + j] = jnp.broadcast_to(w, (nb, CELL))

    def taper(lo_b, hi_b):
        @pl.loop(lo_b, hi_b)
        def _(b):
            at = pl.multiple_of(b * CELL, CELL)
            bx = obx[pl.ds(at, CELL), :]
            by = oby[pl.ds(at, CELL), :]
            for c in range(3):
                for j in range(3):
                    n = c * 3 + j
                    lanes = pl.ds(pl.multiple_of(at + j * CELL, CELL), CELL)
                    d = dist(bx, by, near[c, 16:17, lanes], near[c, 17:18, lanes])
                    rest = 1.0 - jnp.minimum(d, 1.0)
                    r2 = rest * rest
                    v = jnp.exp2(d * (-TAPER_LEN / COV_RANGE * LOG2E))
                    v = v * (r2 * r2) * (5.0 - 4.0 * rest)
                    hi, lo = split(v)
                    ct_hi[n] = hi
                    ct_lo[n] = lo
                    m = near[c, 0:16, lanes] * wv[n, pl.ds(b, 1), :]
                    hi, lo = split(m)
                    vals[0:16, n * CELL : (n + 1) * CELL] = hi
                    vals[16:32, n * CELL : (n + 1) * CELL] = lo
            c_hi = jnp.concatenate([ct_hi[n] for n in range(9)], axis=1)
            c_lo = jnp.concatenate([ct_lo[n] for n in range(9)], axis=1)
            r = lax.dot_general(vals[...], c_hi, NT, preferred_element_type=F32)
            r2 = lax.dot_general(vals[0:16, :], c_lo, NT, preferred_element_type=F32)
            tap[:, pl.ds(at, CELL)] = r[0:16] + r[16:32] + r2

    def bulk(src, dst, ss, rr):
        return copy(src, dst, ss, rr, s, kn[1])

    bulk(near.at[0], near.at[0], h_s.at[0], h_r.at[0]).wait_recv()
    bulk(near.at[2], near.at[2], h_s.at[0], h_r.at[2]).wait_recv()
    h_copies[2].wait_recv()
    h_copies[3].wait_recv()
    taper(0, 3)
    others = [(n, d) for n in range(NK) for d in range(NX) if n or d]
    rest_of = pl.ds(1, NK * NX - 1)
    bulk(rs_src.at[rest_of], rs_dst.at[rest_of], rs_s, rs_r).wait_recv()

    def tree(terms):
        while len(terms) > 1:
            pairs = [a + b for a, b in zip(terms[::2], terms[1::2])]
            terms = pairs + terms[len(terms) & ~1 :]
        return terms[0]

    zb[0] = tree([rs_src[x]] + [rs_dst[n * NX + d] for n, d in others])
    pl.semaphore_wait(relay.at[1], 2)

    def z_copy(d):
        return copy(zb.at[0], zb.at[d], z_s, z_r, zp[d], k)

    for d in sorted(range(1, nz), key=lambda d: -min(d, nz - d)):
        z_copy(d).start()

    loads[5].wait()

    @pl.loop(0, NK)
    def _(i):
        lanes = pl.ds(pl.multiple_of(i * 2 * CELL, 2 * CELL), 2 * CELL)
        hi, lo = split(pf[:, lanes])
        phi[:, lanes] = hi
        plo[:, lanes] = lo

    taper(3, nb)
    low[...] = jnp.zeros((16, rows), F32)
    bulk(kl.at[pl.ds(1, NK - 1)], kl.at[pl.ds(1, NK - 1)], kl_s, kl_r.at[0]).wait_send()
    some = near.at[pl.ds(0, 2), :, pl.ds(CELL, rows)]
    bulk(some, some, h_s.at[0], h_r.at[0]).wait_send()
    some = near.at[:, :, pl.ds(0, 2 * CELL)]
    bulk(some, some, h_s.at[1], h_r.at[0]).wait_send()
    bulk(rs_src.at[rest_of], rs_dst.at[rest_of], rs_s, rs_r).wait_send()
    others_z = zb.at[pl.ds(1, nz - 1)]
    bulk(others_z, others_z, z_s, z_r).wait_recv()
    pj[0] = tree([zb[d] for d in range(nz)])

    def g_copy(n):
        return copy(
            pj.at[0], pj.at[BACK[n]], g_s, g_r.at[BACK[n]], s, kn[n]
        )

    def g_arrival(n):
        return copy(pj.at[0], pj.at[n], g_s, g_r.at[n], s, kn[n])

    for n in (4, 5, 7, 6, 2, 3, 1):
        g_copy(n).start()
    bulk(others_z, others_z, z_s, z_r).wait_send()
    fac = jnp.zeros((4, 2 * CELL), F32)
    for slots in (ARRIVE[:2], ARRIVE[2:6], ARRIVE[6:]):
        for n in slots:
            if n:
                g_arrival(n).wait_recv()
        for n in slots:
            lanes = pl.ds(pl.multiple_of(kn[n] * 2 * CELL, 2 * CELL), 2 * CELL)
            piece = pj[n]
            hi, lo = split(jnp.concatenate([piece[0:4], piece[4:8]], axis=1))
            both = jnp.concatenate([hi.astype(F32), lo.astype(F32)], axis=0)
            both = both.astype(BF16)
            r = lax.dot_general(both, phi[:, lanes], NT, preferred_element_type=F32)
            r2 = lax.dot_general(both, plo[:, lanes], NT, preferred_element_type=F32)
            fac = fac + ((r[0:4] + r[4:8]) + (r2[0:4] + r2[4:8]))
    fb[x, 0:4] = fac[:, 0:CELL]
    fb[x, 4:8] = fac[:, CELL:]

    def f_copy(n, d):
        m = BACK[n]
        return copy(
            fb.at[x], fb.at[m * NX + x], f_s, f_r.at[m], sp[d], kn[n]
        )

    for n in tuple(BACK[m] for m in ARRIVE):
        for d in (2, 1, 3, 0):
            if n or d:
                f_copy(n, d).start()
    bulk(pj.at[pl.ds(1, NK - 1)], pj.at[pl.ds(1, NK - 1)], g_s, g_r.at[0]).wait_send()

    def expand(slots):
        cols, hi_slabs, lo_slabs = [], [], []
        for n in slots:
            for h in range(2):
                part = [fb[n * NX + t, 4 * h : 4 * h + 4] for t in range(NX)]
                cols.append(jnp.concatenate(part, axis=0))
                hi_slabs.append(4 * n + h)
                lo_slabs.append(4 * n + 2 + h)
        hi, lo = split(jnp.concatenate(cols, axis=1))
        both = jnp.concatenate([hi, lo], axis=0)
        k_hi = jnp.concatenate([kk[m] for m in hi_slabs], axis=1)
        k_lo = jnp.concatenate([kk[m] for m in lo_slabs], axis=1)
        r = lax.dot_general(both, k_hi, NT, preferred_element_type=F32)
        r2 = lax.dot_general(hi, k_lo, NT, preferred_element_type=F32)
        low[...] += r[0:16] + r[16:32] + r2

    for n in ARRIVE:
        first_piece = max(n * NX, 1)
        part = fb.at[pl.ds(first_piece, (n + 1) * NX - first_piece)]
        bulk(part, part, f_s, f_r.at[n]).wait_recv()
        expand((n,))

    coef = (
        LOW_SCALE
        * EXPAND_GAIN
        * PROJ_GAIN
        * math.sqrt(NK * 2 * CELL / (ns * NK * rows))
    )

    rest = fb.at[pl.ds(1, NK * NX - 1)]
    bulk(rest, rest, f_s, f_r.at[0]).wait_send()
    out[...] = TAPER_SCALE * tap[...] + coef * low[...] + NUGGET * probes[...]


def shards(probes, locations, knot_locs, knot_precision, neighbours, counts):
    ns = lax.axis_size("space")
    nz = ns // NX
    nb = neighbours.shape[0]
    rows = nb * CELL
    knots = knot_locs.shape[1]
    cols = knots * NK
    alpha = LOG2E / (KNOT_REACH * math.sqrt(nb * ns * NK / cols))
    beta = 1.0 / TAPER_LEN
    dma = pltpu.SemaphoreType.DMA
    applied = pl.pallas_call(
        functools.partial(body, (ns, nz, nb, alpha, beta)),
        out_shape=jax.ShapeDtypeStruct(probes.shape, F32),
        in_specs=[pl.BlockSpec(memory_space=pltpu.HBM)] * 6,
        out_specs=pl.BlockSpec(memory_space=pltpu.VMEM),
        scratch_shapes=[
            pltpu.VMEM((16, rows), F32),
            pltpu.VMEM((2, rows), F32),
            pltpu.VMEM((2, knots), F32),
            pltpu.VMEM((nb, nb), jnp.int32),
            pltpu.SMEM((nb,), jnp.int32),
            pltpu.VMEM((3, 24, rows + 2 * CELL), F32),
            pltpu.VMEM((NK, 8, CELL), F32),
            pltpu.VMEM((rows, CELL), F32),
            pltpu.VMEM((rows, CELL), F32),
            pltpu.VMEM((rows, CELL), F32),
            pltpu.VMEM((rows, CELL), F32),
            pltpu.VMEM((32, rows), BF16),
            pltpu.VMEM((9, nb, CELL), F32),
            pltpu.VMEM((4 * NK, rows, CELL), BF16),
            pltpu.VMEM((32, 4 * CELL), F32),
            pltpu.VMEM((knots, cols), F32),
            pltpu.VMEM((knots, cols), BF16),
            pltpu.VMEM((knots, cols), BF16),
            pltpu.VMEM((NK * NX, 8, CELL), F32),
            pltpu.VMEM((NK * NX, 8, CELL), F32),
            pltpu.VMEM((nz, 8, CELL), F32),
            pltpu.VMEM((NK, 8, CELL), F32),
            pltpu.VMEM((NK * NX, 8, CELL), F32),
            pltpu.VMEM((9, CELL, CELL), BF16),
            pltpu.VMEM((9, CELL, CELL), BF16),
            pltpu.VMEM((32, 9 * CELL), BF16),
            pltpu.VMEM((16, rows), F32),
            pltpu.VMEM((16, rows), F32),
            dma((6,)),
            dma,
            dma((NK,)),
            dma((2,)),
            dma((4,)),
            dma,
            dma,
            dma,
            dma,
            dma,
            dma((NK,)),
            dma,
            dma((NK,)),
            pltpu.SemaphoreType.REGULAR((2,)),
        ],
        compiler_params=pltpu.CompilerParams(
            collective_id=0, has_side_effects=True, vmem_limit_bytes=48 << 20
        ),
    )(*(pltpu.with_memory_space_constraint(a, pltpu.HBM) for a in (probes, locations, knot_locs, knot_precision, neighbours, counts)))
    return applied


def solution(mesh):
    return jax.shard_map(
        shards,
        mesh=mesh,
        in_specs=(
            P(None, ("space", "knot")),
            P(None, ("space", "knot")),
            P(None, "knot"),
            P("knot", None),
            P(("space", "knot"), None),
            P(("space", "knot")),
        ),
        out_specs=P(None, ("space", "knot")),
        check_vma=False,
    )
```

```python
import functools
import math

import jax
import jax.numpy as jnp
from jax import lax
from jax.experimental import pallas as pl
from jax.experimental.pallas import tpu as pltpu
from jax.sharding import PartitionSpec as P

COV_RANGE = 0.05
TAPER_LEN = 0.15
KNOT_REACH = 0.15
TAPER_SCALE = 0.1
PROJ_GAIN = 0.5
EXPAND_GAIN = 0.5
LOW_SCALE = 0.5
NUGGET = 0.25
TINY = 1e-30
LOG2E = 1.0 / math.log(2.0)

NX = 4
NY = 4
CELL = 128
F32 = jnp.float32
BF16 = jnp.bfloat16
NT = (((1,), (1,)), ((), ()))
ORDER = ((0, 0), (0, 1), (3, 1), (1, 1), (2, 1), (2, 0), (1, 0), (3, 0))
STEP = tuple((-dy % NY, dc) for dy, dc in ORDER)
BACK = tuple(ORDER.index(st) for st in STEP)
NK = len(ORDER)
ARRIVE = (0, 1, 7, 2, 6, 3, 5, 4)


def split(v):
    hi = v.astype(BF16)
    return hi, (v - hi.astype(F32)).astype(BF16)


def dist(ax, ay, bx, by):
    dx = ax - bx
    dy = ay - by
    q = dx * dx + dy * dy
    return q * lax.rsqrt(jnp.maximum(q, TINY))


def body(
    cfg,
    probes_hbm,
    locs_hbm,
    knots_hbm,
    prec,
    nbr_hbm,
    cnt_hbm,
    out,
    probes,
    locs,
    knots,
    nbr,
    cnt,
    near,
    kl,
    oax,
    oay,
    obx,
    oby,
    pv,
    wv,
    kk,
    pacc,
    pf,
    phi,
    plo,
    rs_src,
    rs_dst,
    zb,
    pj,
    fb,
    ct_hi,
    ct_lo,
    vals,
    tap,
    in_s,
    kl_s,
    kl_r,
    h_s,
    h_r,
    rs_s,
    rs_r,
    z_s,
    z_r,
    g_s,
    g_r,
    f_s,
    f_r,
    relay,
):
    ns, nz, nb, alpha, beta = cfg
    rows = nb * CELL
    s = lax.axis_index("space")
    k = lax.axis_index("knot")
    x = s // nz
    z = s % nz
    y = k // 2
    core = k % 2

    xs = [x] + [(x + d) % NX for d in range(1, NX)]
    sp = [xx * nz + z for xx in xs]
    zp = [x * nz + (z + d) % nz for d in range(nz)]
    east = ((s + ns - 1) % ns, (s + 1) % ns)
    ys = [y] + [(y + d) % NY for d in range(1, NY)]
    kn = [ys[dy] * 2 + (core + dc) % 2 for dy, dc in ORDER]

    def copy(src, dst, ss, rr, to_s, to_k):
        return pltpu.make_async_remote_copy(
            src_ref=src,
            dst_ref=dst,
            send_sem=ss,
            recv_sem=rr,
            device_id={"space": to_s, "knot": to_k},
            device_id_type=pl.DeviceIdType.MESH,
        )

    def tell(sem, to_s, to_k):
        pl.semaphore_signal(
            sem,
            inc=1,
            device_id={"space": to_s, "knot": to_k},
            device_id_type=pl.DeviceIdType.MESH,
        )

    barrier = pltpu.get_barrier_semaphore()
    for n in range(1, NK):
        tell(barrier, s, kn[n])
    for d in range(1, NX):
        tell(barrier, sp[d], k)
    for to_s in east:
        tell(barrier, to_s, k)
    for d in (1, 2, nz - 1, nz - 2):
        tell(barrier, zp[d], k)
    greeted = NK - 1 + NX - 1 + 2 + 4

    pairs = (
        (knots_hbm, knots),
        (locs_hbm, locs),
        (probes_hbm, probes),
        (nbr_hbm, nbr),
        (cnt_hbm, cnt),
        (prec, pf),
    )
    loads = [pltpu.make_async_copy(a, b, in_s.at[n]) for n, (a, b) in enumerate(pairs)]
    for c in loads:
        c.start()

    kl[0] = jnp.zeros((8, CELL), F32)
    loads[0].wait()
    for h in range(2):
        kl[0, h : h + 1, :] = knots[0:1, h * CELL : (h + 1) * CELL] * alpha
        kl[0, 2 + h : 3 + h, :] = knots[1:2, h * CELL : (h + 1) * CELL] * alpha

    def project(n, at, width):
        lanes = pl.ds(at, width)
        rhs = jnp.concatenate([kk[4 * n + m, lanes, :] for m in range(4)], axis=1)
        return jnp.dot(pv[:, lanes], rhs, preferred_element_type=F32)

    def ship(n, r):
        w = 2 * CELL
        proj = r[0:16, 0:w] + r[16:32, 0:w] + (r[0:16, w:] + r[16:32, w:])
        for t in range(NX):
            for h in range(2):
                rs_src[n * NX + t, 4 * h : 4 * h + 4] = proj[
                    4 * t : 4 * t + 4, CELL * h : CELL * h + CELL
                ]

    def group(n, prev):
        if prev is not None:
            r = project(prev, 0, rows)
        for b in range(nb):
            if n == NK - 1 and b == nb // 2:
                pacc[...] = project(n, 0, rows // 2)
            part = slice(b * CELL, (b + 1) * CELL)
            ax = oax[part, :]
            ay = oay[part, :]
            for h in range(2):
                d = dist(ax, ay, kl[n, h : h + 1, :], kl[n, 2 + h : 3 + h, :])
                hi, lo = split(jnp.exp2(-d))
                kk[4 * n + h, part, :] = hi
                kk[4 * n + 2 + h, part, :] = lo
        if prev is not None:
            ship(prev, r)

    def rs_copy(n, d):
        return copy(
            rs_src.at[n * NX + xs[d]],
            rs_dst.at[n * NX + d],
            rs_s,
            rs_r,
            sp[d],
            kn[n],
        )

    def rs_start(n):
        for d in (2, 1, 3, 0) if n else (2, 1, 3):
            rs_copy(n, d).start()

    def kl_copy(n):
        return copy(
            kl.at[0], kl.at[BACK[n]], kl_s, kl_r.at[BACK[n]], s, kn[n]
        )

    def kl_arrival(n):
        return copy(kl.at[0], kl.at[n], kl_s, kl_r.at[n], s, kn[n])

    near[1, 16:24, CELL : CELL + rows] = jnp.zeros((8, rows), F32)
    loads[1].wait()
    near[1, 16:18, CELL : CELL + rows] = locs[...] * beta
    @pl.loop(0, nb // 2)
    def _(b):
        for u in range(2):
            at = pl.ds(pl.multiple_of(b * 2 * CELL + u * CELL, CELL), CELL)
            cx = jnp.broadcast_to(locs[0:1, at], (CELL, CELL)).T
            cy = jnp.broadcast_to(locs[1:2, at], (CELL, CELL)).T
            oax[at, :] = cx * alpha
            oay[at, :] = cy * alpha
            obx[at, :] = cx * beta
            oby[at, :] = cy * beta

    loads[2].wait()
    near[1, 0:16, CELL : CELL + rows] = probes[...]
    p_hi, p_lo = split(probes[...])
    pv[0:16, :] = p_hi
    pv[16:32, :] = p_lo
    pl.semaphore_wait(barrier, greeted)

    for n in (7, 6, 2, 3, 1, 4, 5):
        kl_copy(n).start()
    for d in range(1, NX):
        tell(relay.at[0], sp[d], k)
    for to_s in east:
        tell(relay.at[0], to_s, k)
    for d in (2, nz - 2):
        tell(relay.at[0], zp[d], k)

    group(0, None)

    mid = (CELL, rows)
    first, last = (CELL, CELL), (rows, CELL)
    below, above = (0, CELL), (rows + CELL, CELL)
    up, down = (k + 1) % NK, (k + NK - 1) % NK
    halo = [
        (east[1], k, mid, 0, mid),
        (east[0], k, mid, 2, mid),
        (s, up, last, 1, below),
        (s, down, first, 1, above),
        (east[1], up, last, 0, below),
        (east[1], down, first, 0, above),
        (east[0], up, last, 2, below),
        (east[0], down, first, 2, above),
    ]
    h_copies = [
        copy(
            near.at[1, :, pl.ds(a, w)],
            near.at[col, :, pl.ds(ta, tw)],
            h_s.at[0 if n < 2 else 1],
            h_r.at[(0, 2, 1, 3, 0, 0, 2, 2)[n]],
            to_s,
            to_k,
        )
        for n, (to_s, to_k, (a, w), col, (ta, tw)) in enumerate(halo)
    ]
    for c in h_copies[:4]:
        c.start()

    kl_arrival(1).wait_recv()
    group(1, 0)
    kl_arrival(2).wait_recv()
    group(2, 1)
    pl.semaphore_wait(relay.at[0], NX - 1 + 2 + 2)
    for d in (4, nz - 4):
        tell(relay.at[1], zp[d], k)
    for c in h_copies[4:]:
        c.start()
    rs_start(0)
    rs_start(1)
    for n in range(3, NK):
        kl_arrival(n).wait_recv()
        group(n, n - 1)
        rs_start(n - 1)
    ship(NK - 1, pacc[...] + project(NK - 1, rows // 2, rows // 2))
    rs_start(NK - 1)

    slot = lax.broadcasted_iota(jnp.int32, (nb, nb), 1)
    row = lax.broadcasted_iota(jnp.int32, (nb, nb), 0)
    loads[3].wait()
    loads[4].wait()
    live = jnp.zeros((nb, nb), jnp.int32)
    for b in range(nb):
        live = jnp.where(row == b, cnt[b], live)
    ids = nbr[...]
    own = s * (NK * nb) + k * nb + row
    for c in range(3):
        for j in range(3):
            hit = (ids == own + (c - 1) * (NK * nb) + (j - 1)) & (slot < live)
            w = jnp.sum(jnp.where(hit, 1.0, 0.0), axis=1, keepdims=True)
            wv[c * 3 + j] = jnp.broadcast_to(w, (nb, CELL))

    def taper(lo_b, hi_b):
        @pl.loop(lo_b, hi_b)
        def _(b):
            at = pl.multiple_of(b * CELL, CELL)
            bx = obx[pl.ds(at, CELL), :]
            by = oby[pl.ds(at, CELL), :]
            for c in range(3):
                for j in range(3):
                    n = c * 3 + j
                    lanes = pl.ds(pl.multiple_of(at + j * CELL, CELL), CELL)
                    d = dist(bx, by, near[c, 16:17, lanes], near[c, 17:18, lanes])
                    rest = 1.0 - jnp.minimum(d, 1.0)
                    r2 = rest * rest
                    v = jnp.exp2(d * (-TAPER_LEN / COV_RANGE * LOG2E))
                    v = v * (r2 * r2) * (5.0 - 4.0 * rest)
                    hi, lo = split(v)
                    ct_hi[n] = hi
                    ct_lo[n] = lo
                    m = near[c, 0:16, lanes] * wv[n, pl.ds(b, 1), :]
                    hi, lo = split(m)
                    vals[0:16, n * CELL : (n + 1) * CELL] = hi
                    vals[16:32, n * CELL : (n + 1) * CELL] = lo
            c_hi = jnp.concatenate([ct_hi[n] for n in range(9)], axis=1)
            c_lo = jnp.concatenate([ct_lo[n] for n in range(9)], axis=1)
            r = lax.dot_general(vals[...], c_hi, NT, preferred_element_type=F32)
            r2 = lax.dot_general(vals[0:16, :], c_lo, NT, preferred_element_type=F32)
            tap[:, pl.ds(at, CELL)] = r[0:16] + r[16:32] + r2

    def bulk(src, dst, ss, rr):
        return copy(src, dst, ss, rr, s, kn[1])

    bulk(near.at[0], near.at[0], h_s.at[0], h_r.at[0]).wait_recv()
    bulk(near.at[2], near.at[2], h_s.at[0], h_r.at[2]).wait_recv()
    h_copies[2].wait_recv()
    h_copies[3].wait_recv()
    taper(0, 3)
    others = [(n, d) for n in range(NK) for d in range(NX) if n or d]
    rest_of = pl.ds(1, NK * NX - 1)
    bulk(rs_src.at[rest_of], rs_dst.at[rest_of], rs_s, rs_r).wait_recv()

    def tree(terms):
        while len(terms) > 1:
            pairs = [a + b for a, b in zip(terms[::2], terms[1::2])]
            terms = pairs + terms[len(terms) & ~1 :]
        return terms[0]

    zb[0] = tree([rs_src[x]] + [rs_dst[n * NX + d] for n, d in others])
    pl.semaphore_wait(relay.at[1], 2)

    def z_copy(d):
        return copy(zb.at[0], zb.at[d], z_s, z_r, zp[d], k)

    for d in sorted(range(1, nz), key=lambda d: -min(d, nz - d)):
        z_copy(d).start()

    loads[5].wait()

    @pl.loop(0, NK)
    def _(i):
        lanes = pl.ds(pl.multiple_of(i * 2 * CELL, 2 * CELL), 2 * CELL)
        hi, lo = split(pf[:, lanes])
        phi[:, lanes] = hi
        plo[:, lanes] = lo

    taper(3, nb)
    out[...] = TAPER_SCALE * tap[...] + NUGGET * probes[...]
    bulk(kl.at[pl.ds(1, NK - 1)], kl.at[pl.ds(1, NK - 1)], kl_s, kl_r.at[0]).wait_send()
    some = near.at[pl.ds(0, 2), :, pl.ds(CELL, rows)]
    bulk(some, some, h_s.at[0], h_r.at[0]).wait_send()
    some = near.at[:, :, pl.ds(0, 2 * CELL)]
    bulk(some, some, h_s.at[1], h_r.at[0]).wait_send()
    bulk(rs_src.at[rest_of], rs_dst.at[rest_of], rs_s, rs_r).wait_send()
    others_z = zb.at[pl.ds(1, nz - 1)]
    bulk(others_z, others_z, z_s, z_r).wait_recv()
    pj[0] = tree([zb[d] for d in range(nz)])

    def g_copy(n):
        return copy(
            pj.at[0], pj.at[BACK[n]], g_s, g_r.at[BACK[n]], s, kn[n]
        )

    def g_arrival(n):
        return copy(pj.at[0], pj.at[n], g_s, g_r.at[n], s, kn[n])

    for n in (4, 5, 7, 6, 2, 3, 1):
        g_copy(n).start()
    bulk(others_z, others_z, z_s, z_r).wait_send()
    fac = jnp.zeros((4, 2 * CELL), F32)
    for slots in (ARRIVE[:2], ARRIVE[2:6], ARRIVE[6:]):
        for n in slots:
            if n:
                g_arrival(n).wait_recv()
        for n in slots:
            lanes = pl.ds(pl.multiple_of(kn[n] * 2 * CELL, 2 * CELL), 2 * CELL)
            piece = pj[n]
            hi, lo = split(jnp.concatenate([piece[0:4], piece[4:8]], axis=1))
            both = jnp.concatenate([hi.astype(F32), lo.astype(F32)], axis=0)
            both = both.astype(BF16)
            r = lax.dot_general(both, phi[:, lanes], NT, preferred_element_type=F32)
            r2 = lax.dot_general(both, plo[:, lanes], NT, preferred_element_type=F32)
            fac = fac + ((r[0:4] + r[4:8]) + (r2[0:4] + r2[4:8]))
    fb[x, 0:4] = fac[:, 0:CELL]
    fb[x, 4:8] = fac[:, CELL:]

    def f_copy(n, d):
        m = BACK[n]
        return copy(
            fb.at[x], fb.at[m * NX + x], f_s, f_r.at[m], sp[d], kn[n]
        )

    for n in tuple(BACK[m] for m in ARRIVE):
        for d in (2, 1, 3, 0):
            if n or d:
                f_copy(n, d).start()
    bulk(pj.at[pl.ds(1, NK - 1)], pj.at[pl.ds(1, NK - 1)], g_s, g_r.at[0]).wait_send()

    coef = (
        LOW_SCALE
        * EXPAND_GAIN
        * PROJ_GAIN
        * math.sqrt(NK * 2 * CELL / (ns * NK * rows))
    )

    def expand(slots):
        cols, hi_slabs, lo_slabs = [], [], []
        for n in slots:
            for h in range(2):
                part = [fb[n * NX + t, 4 * h : 4 * h + 4] for t in range(NX)]
                cols.append(jnp.concatenate(part, axis=0))
                hi_slabs.append(4 * n + h)
                lo_slabs.append(4 * n + 2 + h)
        hi, lo = split(jnp.concatenate(cols, axis=1))
        both = jnp.concatenate([hi, lo], axis=0)
        k_hi = jnp.concatenate([kk[m] for m in hi_slabs], axis=1)
        k_lo = jnp.concatenate([kk[m] for m in lo_slabs], axis=1)
        r = lax.dot_general(both, k_hi, NT, preferred_element_type=F32)
        r2 = lax.dot_general(hi, k_lo, NT, preferred_element_type=F32)
        out[...] += coef * (r[0:16] + r[16:32] + r2)

    for n in ARRIVE:
        first_piece = max(n * NX, 1)
        part = fb.at[pl.ds(first_piece, (n + 1) * NX - first_piece)]
        bulk(part, part, f_s, f_r.at[n]).wait_recv()
        expand((n,))

    rest = fb.at[pl.ds(1, NK * NX - 1)]
    bulk(rest, rest, f_s, f_r.at[0]).wait_send()


def shards(probes, locations, knot_locs, knot_precision, neighbours, counts):
    ns = lax.axis_size("space")
    nz = ns // NX
    nb = neighbours.shape[0]
    rows = nb * CELL
    knots = knot_locs.shape[1]
    cols = knots * NK
    alpha = LOG2E / (KNOT_REACH * math.sqrt(nb * ns * NK / cols))
    beta = 1.0 / TAPER_LEN
    dma = pltpu.SemaphoreType.DMA
    applied = pl.pallas_call(
        functools.partial(body, (ns, nz, nb, alpha, beta)),
        out_shape=jax.ShapeDtypeStruct(probes.shape, F32),
        in_specs=[pl.BlockSpec(memory_space=pltpu.HBM)] * 6,
        out_specs=pl.BlockSpec(memory_space=pltpu.VMEM),
        scratch_shapes=[
            pltpu.VMEM((16, rows), F32),
            pltpu.VMEM((2, rows), F32),
            pltpu.VMEM((2, knots), F32),
            pltpu.VMEM((nb, nb), jnp.int32),
            pltpu.SMEM((nb,), jnp.int32),
            pltpu.VMEM((3, 24, rows + 2 * CELL), F32),
            pltpu.VMEM((NK, 8, CELL), F32),
            pltpu.VMEM((rows, CELL), F32),
            pltpu.VMEM((rows, CELL), F32),
            pltpu.VMEM((rows, CELL), F32),
            pltpu.VMEM((rows, CELL), F32),
            pltpu.VMEM((32, rows), BF16),
            pltpu.VMEM((9, nb, CELL), F32),
            pltpu.VMEM((4 * NK, rows, CELL), BF16),
            pltpu.VMEM((32, 4 * CELL), F32),
            pltpu.VMEM((knots, cols), F32),
            pltpu.VMEM((knots, cols), BF16),
            pltpu.VMEM((knots, cols), BF16),
            pltpu.VMEM((NK * NX, 8, CELL), F32),
            pltpu.VMEM((NK * NX, 8, CELL), F32),
            pltpu.VMEM((nz, 8, CELL), F32),
            pltpu.VMEM((NK, 8, CELL), F32),
            pltpu.VMEM((NK * NX, 8, CELL), F32),
            pltpu.VMEM((9, CELL, CELL), BF16),
            pltpu.VMEM((9, CELL, CELL), BF16),
            pltpu.VMEM((32, 9 * CELL), BF16),
            pltpu.VMEM((16, rows), F32),
            dma((6,)),
            dma,
            dma((NK,)),
            dma((2,)),
            dma((4,)),
            dma,
            dma,
            dma,
            dma,
            dma,
            dma((NK,)),
            dma,
            dma((NK,)),
            pltpu.SemaphoreType.REGULAR((2,)),
        ],
        compiler_params=pltpu.CompilerParams(
            collective_id=0, has_side_effects=True, vmem_limit_bytes=48 << 20
        ),
    )(*(pltpu.with_memory_space_constraint(a, pltpu.HBM) for a in (probes, locations, knot_locs, knot_precision, neighbours, counts)))
    return applied


def solution(mesh):
    return jax.shard_map(
        shards,
        mesh=mesh,
        in_specs=(
            P(None, ("space", "knot")),
            P(None, ("space", "knot")),
            P(None, "knot"),
            P("knot", None),
            P(("space", "knot"), None),
            P(("space", "knot")),
        ),
        out_specs=P(None, ("space", "knot")),
        check_vma=False,
    )
```
